128 devices in a mesh: row: 8 (over y, core), col: 16 (over z, x).
Axes of the slice: x: 4, y: 4, z: 4, core: 2. Of those that a mesh axis runs over, the one named last changes fastest.
Arguments:
- question_vectors: bfloat16 [2048, 2048], P('row', 'col'), may hold values from -0.5 to 0.5
- document_vectors: bfloat16 [2048, 2048], P('col', 'row'), may hold values from -0.5 to 0.5
- positive: int32 [2048], P('row'), may hold values from 0 to 2047
- tokens: bfloat16 [16384, 2048], P(('row', 'col')), may hold values from -6 to 6
- expert_ids: int32 [16384, 8], P(('row', 'col')), may hold values from 0 to 127, all different within a row; in each aligned block of 128 rows (0 to 127, 128 to 255, ...) at most 9 rows name the same one
- route_weights: float32 [16384, 8], P(('row', 'col')), may hold values from 0.03 to 0.3
- expert_gate_up: bfloat16 [128, 2048, 1536], P(('row', 'col')), may hold values from -0.125 to 0.125
- expert_down: bfloat16 [128, 768, 2048], P(('row', 'col')), may hold values from -0.21875 to 0.21875
Outputs:
- passage_grad: float32 [2048, 2048], P('col', 'row')
- token_grad: bfloat16 [16384, 2048], P(('row', 'col'))
- gate_up_grad: bfloat16 [128, 2048, 1536], P(('row', 'col'))
- down_grad: bfloat16 [128, 768, 2048], P(('row', 'col'))
The draws below stay inside these ranges and needn't reach their ends.
Inputs may be any that keep to these rules, and one draw needn't show every extreme that they name: `expert_ids`: each token names 8 different experts; among the 128 tokens of one device no expert is named more than 9 times, a bound that some block reaches.
All inputs are finite; a program needn't handle non-finite values.
Results may differ from the reference program's by a relative error of at most 0.018.
Values may be sent and summed in bfloat16 or wider, within the bound.
No kernel may reach another device: no remote copies, remote signals or barrier semaphores. Data moves between devices by JAX's collectives and lax.ppermute only.
A program may use at most 192 MiB of HBM per device.

```python
import math
import jax
import jax.numpy as jnp
import numpy as np
from jax import lax

D = 2048
FF = 768
TOP = 8
SEQ_LEN = 8
TOK_DEV = 128
TOKENS = 16384
NQ = 2048
NP = 2048
EXPERTS = 128
CAP = 9
DEVICES = 128


sharpness_divisor = 0.02


def embed_pair(key):
    folded = jax.random.fold_in(key, 4099)
    subkeys = jax.random.split(folded, 9)
    question_vectors = jax.random.normal(subkeys[0], (NQ, D), jnp.float32) * 0.03
    document_vectors = jax.random.normal(subkeys[1], (NP, D), jnp.float32) * 0.03
    chosen_q = jax.random.permutation(subkeys[4], NQ)[:8]
    chosen_p = jax.random.permutation(subkeys[5], NP)[:16]
    sign_pattern = jax.random.randint(subkeys[6], (8, D), 0, 2).astype(jnp.float32) * 2.0 - 1.0
    direction_unit = sign_pattern / math.sqrt(D)
    correct_classes = jnp.array([110.0, 170.0, 230.0, 290.0, 140.0, 200.0, 260.0, 320.0], jnp.float32)
    magnitude = jnp.sqrt(correct_classes * sharpness_divisor)[:, None]
    query_planted = magnitude * direction_unit
    passage_planted = magnitude * direction_unit
    interval_lengths = jax.random.uniform(subkeys[7], (8,), jnp.float32, 1.0, 3.0)
    query_power = jnp.sum(query_planted * query_planted, axis=1, keepdims=True)
    jitter_shift = jax.random.normal(subkeys[8], (8, D), jnp.float32) * (0.2 / math.sqrt(D))
    jitter_shift = jitter_shift - jnp.sum(jitter_shift * query_planted, axis=1, keepdims=True) / query_power * query_planted
    distractor_vector = passage_planted - interval_lengths[:, None] * sharpness_divisor * query_planted / query_power + jitter_shift
    question_vectors = question_vectors.at[chosen_q].set(query_planted)
    document_vectors = document_vectors.at[chosen_p[:8]].set(passage_planted)
    document_vectors = document_vectors.at[chosen_p[8:]].set(distractor_vector)
    return (jnp.clip(question_vectors, -0.5, 0.5), jnp.clip(document_vectors, -0.5, 0.5))


def draw_question_vectors(key, part):
    return embed_pair(key)[0].astype(jnp.bfloat16)


def draw_document_vectors(key, part):
    return embed_pair(key)[1].astype(jnp.bfloat16)


def touch_ends(entries, stream_key, least, top_value):
    longest = entries.shape.index(max(entries.shape))
    spots = []
    for shift in (0, 1):
        where = [jax.random.randint(jax.random.fold_in(stream_key, axis), (), 0, length) for axis, length in enumerate(entries.shape)]
        where[longest] = (where[longest] + shift) % entries.shape[longest]
        spots.append(tuple(where))
    return entries.at[spots[0]].set(least).at[spots[1]].set(top_value)


def block_levels(key, shape, cuts, smallest, largest):
    loudness = 1.0
    for dim, blocks in cuts:
        steps = jax.random.uniform(jax.random.fold_in(jax.random.fold_in(key, 6), dim), (blocks,), jnp.float32, smallest / len(cuts), largest / len(cuts))
        loudness = loudness * jnp.repeat(jnp.exp(steps), shape[dim] // blocks).reshape((-1,) + (1,) * (len(shape) - 1 - dim))
    return loudness


def routed_block(rng, own, number, rows, amount, top, limit, skew):
    order = jax.random.permutation(rng, amount)
    crowded, usual = shares(amount, rows * top, limit, skew, True), shares(amount, rows * top, limit, skew, False)
    places = jnp.arange(amount)

    def named(tallies, offset_by):
        used = int((tallies > 0).sum())
        fixed = max(1, used // 4)
        shifted = fixed + (places - fixed + offset_by * (used - fixed)) % max(1, amount - fixed)
        return jnp.zeros((amount,), jnp.int32).at[order[jnp.where(places < fixed, places, shifted)]].set(jnp.asarray(tallies, jnp.int32))

    tallies = jnp.where(number % 4 == 0, named(crowded, number // 4), named(usual, number - number // 4 - 1))
    mixed = jax.random.permutation(jax.random.fold_in(own, 3), amount)
    donor, receiver = mixed[0:amount // 2 * 2:2], mixed[1:amount // 2 * 2:2]
    margin = jnp.minimum(tallies[donor] - 1, limit - tallies[receiver]) // 2
    margin = jnp.where((donor == order[0]) | (receiver == order[0]) | (tallies[receiver] == 0), 0, jnp.maximum(margin, 0))
    shifted = jax.random.randint(jax.random.fold_in(own, 4), (amount // 2,), 0, 1 << 20) % (margin + 1)
    tallies = tallies.at[donor].add(-shifted).at[receiver].add(shifted)
    members = jnp.searchsorted(jnp.cumsum(tallies), jnp.arange(rows * top), side="right").astype(jnp.int32)
    table = members.reshape(top, rows).T
    table = table[jax.random.permutation(jax.random.fold_in(own, 1), rows)]
    offset_by = jax.random.randint(jax.random.fold_in(own, 2), (rows, 1), 0, top)
    return jnp.take_along_axis(table, (jnp.arange(top)[None, :] + offset_by) % top, axis=1)


def shares(amount, total, limit, skew, full):
    weights = [(1 << 20) // math.isqrt(grade ** skew) + 1 for grade in range(1, amount + 1)]
    largest = limit if full else min(limit, max(-(-total // amount), total * weights[0] // sum(weights)))
    least = 1 if total - largest >= amount - 1 else 0
    counts, spare = [largest] + [least] * (amount - 1), total - largest - least * (amount - 1)
    while spare > 0:
        candidates = [i for i in range(1, amount) if counts[i] < largest] or [i for i in range(1, amount) if counts[i] < limit]
        whole, budget = sum([weights[i] for i in candidates]), spare
        for i in candidates:
            extra = min(limit - counts[i], max(1, budget * weights[i] // whole), spare)
            counts[i] = counts[i] + extra
            spare = spare - extra
    return np.array(counts)


def gaussian(own_key, extent, scale, most, pieces=(), held_as=jnp.bfloat16):
    values = scale * jax.random.normal(own_key, extent, jnp.float32)
    if pieces:
        values = values * block_levels(own_key, extent, pieces, -0.22, 0.18)
    return jnp.clip(values, -most, most).astype(held_as)


def setup_inputs(seed: int = 0) -> dict:
    key_list = jax.random.split(jax.random.key(seed), 9)
    question_vectors = draw_question_vectors(jax.random.fold_in(key_list[8], 71), 0)
    document_vectors = draw_document_vectors(jax.random.fold_in(key_list[8], 71), 0)
    positive = touch_ends(jax.random.randint(key_list[2], (NQ,), 0, NP), jax.random.fold_in(key_list[2], 1), 0, NP - 1).astype(jnp.int32)
    tokens = gaussian(key_list[3], (TOKENS, D), 1.0, 6.0, ((0, 128),))
    expert_ids_keys = jax.random.split(jax.random.fold_in(key_list[4], 1), TOKENS // TOK_DEV)
    expert_ids_turns = jax.random.permutation(jax.random.fold_in(key_list[4], 3), TOKENS // TOK_DEV)
    expert_ids = jax.vmap(lambda own, number: routed_block(jax.random.fold_in(key_list[4], 2), own, number, TOK_DEV, EXPERTS, TOP, CAP, 1))(expert_ids_keys, expert_ids_turns).reshape((TOKENS, TOP))
    route_weights = jnp.clip(jnp.exp(math.log(0.3) - 2.3025852 * jax.random.uniform(key_list[5], (TOKENS, TOP), jnp.float32) ** block_levels(key_list[5], (TOKENS, TOP), ((0, 128),), -0.2, 0.2)), 0.03, 0.3)
    expert_gate_up = gaussian(key_list[6], (EXPERTS, D, 2 * FF), D ** -0.5, 0.125, ((0, 128),))
    expert_down = gaussian(key_list[7], (EXPERTS, FF, D), FF ** -0.5, 0.21875, ((0, 128),))
    return dict(question_vectors=question_vectors, document_vectors=document_vectors, positive=positive, tokens=tokens, expert_ids=expert_ids, route_weights=route_weights, expert_gate_up=expert_gate_up, expert_down=expert_down)


sharpness_divisor = 0.02


def expert_backward(slot_inputs, slot_grads, gate_up, down_proj):
    projected = jnp.dot(slot_inputs, gate_up, preferred_element_type=jnp.float32)
    hidden_width = down_proj.shape[0]
    gate_part = projected[:, :hidden_width]
    up_part = projected[:, hidden_width:]
    sigmoid_gate = jax.nn.sigmoid(gate_part)
    activated = gate_part * sigmoid_gate
    hidden = (activated * up_part).astype(jnp.bfloat16)
    down_grad = lax.dot_general(hidden, slot_grads, (((0,), (0,)), ((), ())), preferred_element_type=jnp.float32).astype(jnp.bfloat16)
    hidden_grad = lax.dot_general(slot_grads, down_proj, (((1,), (1,)), ((), ())), preferred_element_type=jnp.float32)
    slope = sigmoid_gate * (1.0 + gate_part * (1.0 - sigmoid_gate))
    pre_grad = jnp.concatenate([hidden_grad * up_part * slope, hidden_grad * activated], axis=1).astype(jnp.bfloat16)
    gate_up_grad = lax.dot_general(slot_inputs, pre_grad, (((0,), (0,)), ((), ())), preferred_element_type=jnp.float32).astype(jnp.bfloat16)
    input_grad = lax.dot_general(pre_grad, gate_up, (((1,), (1,)), ((), ())), preferred_element_type=jnp.float32).astype(jnp.bfloat16)
    return input_grad, gate_up_grad, down_grad


def reference(question_vectors, document_vectors, positive, tokens, expert_ids, route_weights, expert_gate_up, expert_down):
    similarity_entries = jnp.dot(question_vectors, document_vectors.T, preferred_element_type=jnp.float32) / sharpness_divisor
    row_peak = jnp.max(similarity_entries, axis=1, keepdims=True)
    coefficient_entries = jnp.exp(similarity_entries - row_peak)
    partition_normalizer = jnp.sum(coefficient_entries, axis=1, keepdims=True)
    columns = jnp.arange(NP, dtype=jnp.int32)
    membership_table = (positive[:, None] == columns[None, :]).astype(jnp.float32)
    similarity_derivative = ((coefficient_entries / partition_normalizer - membership_table) / sharpness_divisor).astype(jnp.bfloat16)
    query_grad = jnp.dot(similarity_derivative, document_vectors, preferred_element_type=jnp.float32)
    passage_grad = jnp.dot(similarity_derivative.T, question_vectors, preferred_element_type=jnp.float32)
    cotangent = jnp.repeat(query_grad / SEQ_LEN, SEQ_LEN, axis=0).astype(jnp.bfloat16)

    blocks = expert_ids.reshape(DEVICES, TOK_DEV * TOP)
    expert_hit = (blocks[:, :, None] == jnp.arange(EXPERTS, dtype=jnp.int32)[None, None, :]).astype(jnp.int32)
    before = jnp.cumsum(expert_hit, axis=1) - expert_hit
    slot_number = jnp.sum(before * expert_hit, axis=2)
    source = jnp.arange(DEVICES, dtype=jnp.int32)[:, None]
    slot_index = (blocks * (DEVICES * CAP) + source * CAP + slot_number).reshape(-1).astype(jnp.int32)
    slot_owner = jnp.full((EXPERTS * DEVICES * CAP,), -1, jnp.int32)
    slot_owner = slot_owner.at[slot_index].set(jnp.arange(TOKENS * TOP, dtype=jnp.int32))
    slot_owner = slot_owner.reshape(EXPERTS, DEVICES * CAP)
    flat_weights = route_weights.reshape(-1)

    def per_expert(carried, inputs):
        owners, gate_up, down_proj = inputs
        filled = owners >= 0
        pair_row = jnp.maximum(owners, 0).astype(jnp.int32)
        token_row = (pair_row // TOP).astype(jnp.int32)
        slot_inputs = jnp.where(filled[:, None], tokens[token_row], jnp.zeros((), tokens.dtype))
        scaled = jnp.where(filled, flat_weights[pair_row], jnp.zeros((), flat_weights.dtype))
        slot_grads = (scaled[:, None] * cotangent[token_row].astype(jnp.float32)).astype(jnp.bfloat16)
        input_grad, gate_up_grad, down_grad = expert_backward(slot_inputs, slot_grads, gate_up, down_proj)
        addend = jnp.where(filled[:, None], input_grad.astype(jnp.float32), jnp.zeros((), jnp.float32))
        carried = carried.at[token_row].add(addend)
        return carried, (gate_up_grad, down_grad)

    start_grad = jnp.zeros((TOKENS, D), jnp.float32)
    summed, (gate_up_grad, down_grad) = lax.scan(per_expert, start_grad, (slot_owner, expert_gate_up, expert_down))
    token_grad = (cotangent.astype(jnp.float32) + summed).astype(jnp.bfloat16)
    return passage_grad, token_grad, gate_up_grad, down_grad
```

```python
import functools
import jax
import jax.numpy as jnp
from jax import lax
from jax.experimental import pallas as pl
from jax.experimental.pallas import tpu as pltpu
from jax.sharding import PartitionSpec as P

SEQ_LEN = 8
SHARPNESS = 0.02
MAIN = 8
LANES = 128
B16 = jnp.bfloat16
F32 = jnp.float32
VMEM_LIMIT = 56 * 1024 * 1024


def iota(shape, dim):
    return lax.broadcasted_iota(jnp.int32, shape, dim)


def params():
    return pltpu.CompilerParams(vmem_limit_bytes=VMEM_LIMIT)


def whole(shape):
    zeros = (0,) * len(shape)
    return pl.BlockSpec(shape, lambda *_: zeros, pipeline_mode=pl.Buffered(1))


def dot(a, b, dims=((1,), (0,))):
    return lax.dot_general(a, b, (dims, ((), ())), preferred_element_type=F32)


def one_hot(mask):
    return jnp.where(mask, 1.0, 0.0).astype(B16)


def slot_keys(ids_t, experts):
    toks = ids_t.shape[1]
    expert = iota((experts, toks), 0)
    hit = jnp.zeros((experts, toks), F32)
    for k in range(ids_t.shape[0]):
        hit += jnp.where(ids_t[k : k + 1, :] == expert, 1.0, 0.0)
    earlier = one_hot(iota((toks, toks), 0) < iota((toks, toks), 1))
    rank = dot(hit.astype(B16), earlier)
    return jnp.where(hit > 0.0, rank, -1.0).astype(jnp.int32)


def per_slot(value):
    experts, toks = value.shape
    return jnp.broadcast_to(value[:, None, :], (experts, MAIN, toks)).reshape(
        experts * MAIN, toks
    )


def send_tokens_kernel(ids_ref, tok_ref, out_ref, key_ref):
    j = pl.program_id(0)
    tiles = pl.num_programs(0) - 1
    width = out_ref.shape[1]
    experts = out_ref.shape[0] // MAIN

    @pl.when(j == 0)
    def _():
        key_ref[...] = per_slot(slot_keys(ids_ref[...], experts))

    slot = iota(key_ref.shape, 0) % MAIN

    @pl.when(j < tiles)
    def _():
        cols = pl.ds(pl.multiple_of(j * width, width), width)
        out_ref[...] = dot(one_hot(key_ref[...] == slot), tok_ref[:, cols]).astype(B16)

    @pl.when(j == tiles)
    def _():
        ninth = key_ref[...] == MAIN
        total = jnp.zeros(out_ref.shape, F32)
        for i in range(MAIN):
            total += dot(one_hot(ninth & (slot == i)), tok_ref[:, i * width : (i + 1) * width])
        out_ref[...] = total.astype(B16)


def send_tokens(ids_t, tokens, experts):
    toks, depth = tokens.shape
    width = depth // MAIN
    return pl.pallas_call(
        send_tokens_kernel,
        grid=(MAIN + 1,),
        in_specs=[whole(ids_t.shape), whole(tokens.shape)],
        out_specs=pl.BlockSpec((experts * MAIN, width), lambda j: (0, j)),
        out_shape=jax.ShapeDtypeStruct((experts * MAIN, depth + width), B16),
        scratch_shapes=[pltpu.VMEM((experts * MAIN, toks), jnp.int32)],
        compiler_params=params(),
        name="send_tokens",
    )(ids_t, tokens)


def send_grads_kernel(ids_ref, weight_ref, part_ref, out_ref, cot_ref, key_ref, row_ref, rep_ref):
    j = pl.program_id(0)
    tiles = pl.num_programs(0) - 1
    width = out_ref.shape[1]
    experts = out_ref.shape[0] // MAIN
    slots, toks = key_ref.shape

    @pl.when(j == 0)
    def _():
        ids = ids_ref[...]
        key = per_slot(slot_keys(ids, experts))
        key_ref[...] = key
        expert = iota((experts, toks), 0)
        weight = jnp.zeros((experts, toks), F32)
        for k in range(ids.shape[0]):
            weight += jnp.where(ids[k : k + 1, :] == expert, weight_ref[k : k + 1, :], 0.0)
        weight = per_slot(weight)
        slot = iota((slots, toks), 0) % MAIN
        main = jnp.sum(jnp.where(key == slot, weight, 0.0), axis=1, keepdims=True)
        ninth = jnp.sum(jnp.where(key == MAIN, weight, 0.0), axis=1, keepdims=True)
        row_ref[...] = jnp.where(iota(row_ref.shape, 1) == 0, main, ninth)
        total = part_ref[0].astype(F32)
        for c in range(1, part_ref.shape[0]):
            total += part_ref[c].astype(F32)
        cot = (total / SEQ_LEN).astype(B16)
        cot_ref[...] = cot
        spread = one_hot(iota((toks, cot.shape[0]), 0) // SEQ_LEN == iota((toks, cot.shape[0]), 1))
        rep_ref[...] = dot(spread, cot).astype(B16)

    slot = iota((slots, toks), 0) % MAIN

    @pl.when(j < tiles)
    def _():
        cols = pl.ds(pl.multiple_of(j * width, width), width)
        rows = dot(one_hot(key_ref[...] == slot), rep_ref[:, cols])
        out_ref[...] = (rows * row_ref[:, 0:1]).astype(B16)

    @pl.when(j == tiles)
    def _():
        ninth = key_ref[...] == MAIN
        total = jnp.zeros(out_ref.shape, F32)
        for i in range(MAIN):
            total += dot(one_hot(ninth & (slot == i)), rep_ref[:, i * width : (i + 1) * width])
        out_ref[...] = (total * row_ref[:, 1:2]).astype(B16)


def send_grads(ids_t, weights_t, parts, experts):
    toks = ids_t.shape[1]
    _, queries, depth = parts.shape
    width = depth // MAIN
    return pl.pallas_call(
        send_grads_kernel,
        grid=(MAIN + 1,),
        in_specs=[whole(ids_t.shape), whole(weights_t.shape), whole(parts.shape)],
        out_specs=[
            pl.BlockSpec((experts * MAIN, width), lambda j: (0, j)),
            pl.BlockSpec((queries, depth), lambda j: (0, 0)),
        ],
        out_shape=[
            jax.ShapeDtypeStruct((experts * MAIN, depth + width), B16),
            jax.ShapeDtypeStruct((queries, depth), B16),
        ],
        scratch_shapes=[
            pltpu.VMEM((experts * MAIN, toks), jnp.int32),
            pltpu.VMEM((experts * MAIN, 128), F32),
            pltpu.VMEM((toks, depth), B16),
        ],
        compiler_params=params(),
        name="send_grads",
    )(ids_t, weights_t, parts)


def unfold(fold, fold_ref, out_ref):
    sources, depth = out_ref.shape
    width = depth // MAIN
    for half in range(width // LANES):
        at = slice(half * LANES, (half + 1) * LANES)
        fold_ref[half] = fold[:, at].astype(F32)
        for i in range(MAIN):
            piece = fold_ref[half, pl.ds(i, sources, stride=MAIN), :]
            start = i * width + half * LANES
            out_ref[:, start : start + LANES] = piece.astype(B16)


def forward_kernel(x_ref, gate_ref, up_ref, hid_ref, cg_ref, cu_ref, x9_ref, fold_ref):
    j = pl.program_id(0)
    depth = gate_ref.shape[0]
    rows = x_ref.shape[0]

    @pl.when(j == 0)
    def _():
        unfold(x_ref[:, depth:], fold_ref, x9_ref)

    def finish(at, gate, up):
        sig = 1.0 / (1.0 + jnp.exp(-gate))
        act = gate * sig
        hid_ref[at, :] = (act * up).astype(B16)
        cg_ref[at, :] = (up * (sig * (1.0 + gate * (1.0 - sig)))).astype(B16)
        cu_ref[at, :] = act.astype(B16)

    step = rows // 4
    for m in range(4):
        x = x_ref[m * step : (m + 1) * step, :depth]
        finish(slice(m * step, (m + 1) * step), dot(x, gate_ref[...]), dot(x, up_ref[...]))
    x = x9_ref[...]
    finish(slice(rows, hid_ref.shape[0]), dot(x, gate_ref[...]), dot(x, up_ref[...]))


def forward(x, gate_up, hidden):
    rows, _ = x.shape
    depth = gate_up.shape[0]
    sources = rows // MAIN
    tile = 256
    tiles = hidden // tile
    col = lambda j: (0, j)
    part = pl.BlockSpec((rows + sources, tile), col)
    shape = jax.ShapeDtypeStruct((rows + sources, hidden), B16)
    return pl.pallas_call(
        forward_kernel,
        grid=(tiles,),
        in_specs=[
            whole(x.shape),
            pl.BlockSpec((depth, tile), col),
            pl.BlockSpec((depth, tile), lambda j: (0, j + tiles)),
        ],
        out_specs=[part, part, part, pl.BlockSpec((sources, depth), lambda j: (0, 0))],
        out_shape=[shape, shape, shape, jax.ShapeDtypeStruct((sources, depth), B16)],
        scratch_shapes=[pltpu.VMEM((depth // MAIN // LANES, rows, LANES), F32)],
        compiler_params=params(),
        cost_estimate=pl.CostEstimate(
            flops=2 * (rows + sources) * depth * 2 * hidden,
            bytes_accessed=2 * (x.size + gate_up.size + 3 * (rows + sources) * hidden),
            transcendentals=(rows + sources) * hidden,
        ),
        name="expert_forward",
    )(x, gate_up, gate_up)


def backward_kernel(
    first, g_ref, down_ref, cg_ref, cu_ref, w_ref, out_ref, pg_ref, g9_ref, fold_ref
):
    j = pl.program_id(0)
    rows = g_ref.shape[0]
    sources, depth = g9_ref.shape
    width = out_ref.shape[1]
    total = rows + sources
    tile = down_ref.shape[0]
    hidden = pg_ref.shape[1] // 2

    @pl.when(j == 0)
    def _():
        unfold(g_ref[:, depth:], fold_ref, g9_ref)

    @pl.when(j < first)
    def _():
        def finish(at, grad):
            gate_cols = pl.ds(pl.multiple_of(j * tile, tile), tile)
            up_cols = pl.ds(pl.multiple_of(hidden + j * tile, tile), tile)
            pg_ref[at, gate_cols] = (grad * cg_ref[at, :].astype(F32)).astype(B16)
            pg_ref[at, up_cols] = (grad * cu_ref[at, :].astype(F32)).astype(B16)

        step = rows // 4
        for m in range(4):
            at = slice(m * step, (m + 1) * step)
            finish(at, dot(g_ref[at, :depth], down_ref[...], ((1,), (1,))))
        finish(slice(rows, total), dot(g9_ref[...], down_ref[...], ((1,), (1,))))

    @pl.when((j >= first) & (j < first + MAIN))
    def _():
        step = rows // 4
        for m in range(4):
            at = slice(m * step, (m + 1) * step)
            out_ref[at, :] = dot(pg_ref[at, :], w_ref[...], ((1,), (1,))).astype(B16)
        ninth = dot(pg_ref[rows:total, :], w_ref[...], ((1,), (1,)))
        for half in range(width // LANES):
            fold_ref[half, pl.ds(j - first, sources, stride=MAIN), :] = ninth[
                :, half * LANES : (half + 1) * LANES
            ]

    @pl.when(j == first + MAIN)
    def _():
        for half in range(width // LANES):
            out_ref[:, half * LANES : (half + 1) * LANES] = fold_ref[half].astype(B16)


def backward(g, down, cg, cu, gate_up):
    rows, _ = g.shape
    hidden, depth = down.shape
    sources = rows // MAIN
    width = depth // MAIN
    tile = 256
    first = hidden // tile
    head = lambda j: (0, jnp.minimum(j, first - 1))
    part = pl.BlockSpec((rows + sources, tile), head)
    return pl.pallas_call(
        functools.partial(backward_kernel, first),
        grid=(first + MAIN + 1,),
        in_specs=[
            whole(g.shape),
            pl.BlockSpec((tile, depth), lambda j: (jnp.minimum(j, first - 1), 0)),
            part,
            part,
            pl.BlockSpec(
                (width, 2 * hidden), lambda j: (jnp.clip(j - first, 0, MAIN - 1), 0)
            ),
        ],
        out_specs=[
            pl.BlockSpec((rows, width), lambda j: (0, jnp.maximum(j - first, 0))),
            pl.BlockSpec((rows + sources, 2 * hidden), lambda j: (0, 0)),
            pl.BlockSpec((sources, depth), lambda j: (0, 0)),
        ],
        out_shape=[
            jax.ShapeDtypeStruct((rows, depth + width), B16),
            jax.ShapeDtypeStruct((rows + sources, 2 * hidden), B16),
            jax.ShapeDtypeStruct((sources, depth), B16),
        ],
        scratch_shapes=[pltpu.VMEM((width // LANES, rows, LANES), F32)],
        compiler_params=params(),
        cost_estimate=pl.CostEstimate(
            flops=6 * (rows + sources) * depth * hidden,
            bytes_accessed=2 * (2 * g.size + down.size + gate_up.size),
            transcendentals=0,
        ),
        name="expert_backward",
    )(g, down, cg, cu, gate_up)


def weight_grad_kernel(a_ref, a9_ref, b_ref, b9_ref, out_ref):
    rows = b_ref.shape[0]
    width = out_ref.shape[0]
    out_ref[...] = (
        dot(a_ref[:, :width], b_ref[...], ((0,), (0,))) + dot(a9_ref[...], b9_ref[...], ((0,), (0,)))
    ).astype(B16)


def weight_grad(a, a9, b, b9, columns, a9_block, b9_block, name):
    sources = a9.shape[0] if a9_block == 0 else a.shape[0] - 8 * (a.shape[0] // 9)
    rows = sources * MAIN
    width = a9.shape[1]
    tile = 256
    return pl.pallas_call(
        weight_grad_kernel,
        grid=(columns // tile,),
        in_specs=[
            pl.BlockSpec((rows, a.shape[1]), lambda j: (0, 0), pipeline_mode=pl.Buffered(1)),
            pl.BlockSpec(
                (sources, width), lambda j: (a9_block, 0), pipeline_mode=pl.Buffered(1)
            ),
            pl.BlockSpec((rows, tile), lambda j: (0, j)),
            pl.BlockSpec((sources, tile), lambda j: (b9_block, j)),
        ],
        out_specs=pl.BlockSpec((width, tile), lambda j: (0, j)),
        out_shape=jax.ShapeDtypeStruct((width, columns), B16),
        compiler_params=params(),
        cost_estimate=pl.CostEstimate(
            flops=2 * 9 * sources * width * columns,
            bytes_accessed=2 * (9 * sources * (width + columns) + width * columns),
            transcendentals=0,
        ),
        name=name,
    )(a, a9, b, b9)


def combine_kernel(ids_ref, cot_ref, got_ref, fold_ref, out_ref, key_ref):
    j = pl.program_id(0)
    toks, slots = key_ref.shape
    experts = slots // MAIN

    @pl.when(j == 0)
    def _():
        ids = ids_ref[...]
        expert = iota((toks, experts), 1)
        hit = jnp.zeros((toks, experts), F32)
        for k in range(ids.shape[1]):
            hit += jnp.where(ids[:, k : k + 1] == expert, 1.0, 0.0)
        earlier = one_hot(iota((toks, toks), 1) < iota((toks, toks), 0))
        rank = dot(earlier, hit.astype(B16))
        key = jnp.where(hit > 0.0, rank, -1.0).astype(B16)
        spread = one_hot(iota((experts, slots), 0) == iota((experts, slots), 1) // MAIN)
        key_ref[...] = dot(key, spread).astype(jnp.int32)

    key = key_ref[...]
    slot = iota(key.shape, 1) % MAIN
    queries = cot_ref.shape[0]
    spread = one_hot(iota((toks, queries), 0) // SEQ_LEN == iota((toks, queries), 1))
    total = dot(one_hot(key == slot), got_ref[...])
    total += dot(one_hot((key == MAIN) & (slot == j)), fold_ref[...])
    out_ref[...] = (dot(spread, cot_ref[...]) + total).astype(B16)


def combine(ids, cot, got):
    toks = ids.shape[0]
    queries, depth = cot.shape
    rows = got.shape[0]
    width = depth // MAIN
    return pl.pallas_call(
        combine_kernel,
        grid=(MAIN,),
        in_specs=[
            whole(ids.shape),
            pl.BlockSpec((queries, width), lambda j: (0, j)),
            pl.BlockSpec((rows, width), lambda j: (0, j)),
            pl.BlockSpec((rows, width), lambda j: (0, MAIN), pipeline_mode=pl.Buffered(1)),
        ],
        out_specs=pl.BlockSpec((toks, width), lambda j: (0, j)),
        out_shape=jax.ShapeDtypeStruct((toks, depth), B16),
        scratch_shapes=[pltpu.VMEM((toks, rows), jnp.int32)],
        compiler_params=params(),
        name="combine",
    )(ids, cot, got, got)


def sent_to_all(value, axis):
    peers = lax.axis_size(axis)
    return lax.all_to_all(
        jnp.broadcast_to(value[None], (peers, *value.shape)), axis, 0, 0, tiled=True
    )


def gathered_copies(value, axis):
    tiles = jnp.moveaxis(sent_to_all(value, axis), 0, 1)
    return tiles.reshape(tiles.shape[0], -1)


def split_up(value, dim, peers):
    lengths = value.shape
    tiles = value.reshape(*lengths[:dim], peers, lengths[dim] // peers, *lengths[dim + 1 :])
    return jnp.moveaxis(tiles, dim, 0)


def exchanged(block, experts):
    rows, width = block.shape
    got = lax.all_to_all(
        block.reshape(experts, rows // experts, width), ("row", "col"), 0, 0, tiled=True
    )
    return got.reshape(rows, width)


def shards(
    question_vectors,
    document_vectors,
    positive,
    tokens,
    expert_ids,
    route_weights,
    expert_gate_up,
    expert_down,
):
    row_size = lax.axis_size("row")
    col_size = lax.axis_size("col")
    experts = row_size * col_size
    gate_up, down = expert_gate_up[0], expert_down[0]
    hidden = down.shape[0]

    ids_t, weights_t = expert_ids.T, route_weights.T
    tokens_out = send_tokens(ids_t, tokens, experts)

    passages = gathered_copies(document_vectors, "row")
    queries = gathered_copies(question_vectors, "col")
    scores = dot(queries, passages, ((1,), (1,))) / SHARPNESS
    local_peak = jnp.max(scores, axis=1)
    local_total = jnp.sum(jnp.exp(scores - local_peak[:, None]), axis=1)
    stats = sent_to_all(jnp.stack([local_peak, local_total]), "col")
    peak = jnp.max(stats[:, 0], axis=0)
    total = jnp.sum(stats[:, 1] * jnp.exp(stats[:, 0] - peak[None]), axis=0)
    count = passages.shape[0]
    columns = lax.axis_index("col") * count + jnp.arange(count, dtype=jnp.int32)
    chosen = (positive[:, None] == columns[None, :]).astype(F32)
    dscore = ((jnp.exp(scores - peak[:, None]) / total[:, None] - chosen) / SHARPNESS).astype(B16)
    query_part = dot(dscore, passages).astype(B16)
    query_parts = lax.all_to_all(split_up(query_part, 0, col_size), "col", 0, 0, tiled=True)

    slot_inputs = exchanged(tokens_out, experts)
    grads_out, cot = send_grads(ids_t, weights_t, query_parts, experts)
    slot_grads = exchanged(grads_out, experts)

    passage_part = dot(dscore, queries, ((0,), (0,))).astype(B16)
    passage_parts = lax.all_to_all(split_up(passage_part, 1, row_size), "row", 0, 0, tiled=True)
    passage_grad = jnp.sum(passage_parts.astype(F32), axis=0)

    hid, cg, cu, inputs9 = forward(slot_inputs, gate_up, hidden)
    back_out, pre_grad, grads9 = backward(slot_grads, down, cg, cu, gate_up)
    returned = exchanged(back_out, experts)
    down_grad = weight_grad(hid, hid, slot_grads, grads9, down.shape[1], MAIN, 0, "down_grad")
    gate_up_grad = weight_grad(
        slot_inputs, inputs9, pre_grad, pre_grad, 2 * hidden, 0, MAIN, "gate_up_grad"
    )
    token_grad = combine(expert_ids, cot, returned)
    return (passage_grad, token_grad, gate_up_grad[None], down_grad[None])


def solution(mesh):
    in_specs = (
        P("row", "col"),
        P("col", "row"),
        P("row"),
        P(("row", "col"), None),
        P(("row", "col"), None),
        P(("row", "col"), None),
        P(("row", "col"), None, None),
        P(("row", "col"), None, None),
    )
    out_specs = (
        P("col", "row"),
        P(("row", "col"), None),
        P(("row", "col"), None, None),
        P(("row", "col"), None, None),
    )
    return jax.shard_map(shards, mesh=mesh, in_specs=in_specs, out_specs=out_specs, check_vma=False)
```

```python
import functools
import math

import jax
import jax.numpy as jnp
from jax import lax
from jax.experimental import pallas as pl
from jax.experimental.pallas import tpu as pltpu
from jax.sharding import PartitionSpec as P

SEQ_LEN = 8
SHARPNESS = 0.02
MAIN = 8
LANES = 128
B16 = jnp.bfloat16
F32 = jnp.float32
VMEM_LIMIT = 56 * 1024 * 1024


def iota(shape, dim):
    return lax.broadcasted_iota(jnp.int32, shape, dim)


def params():
    return pltpu.CompilerParams(vmem_limit_bytes=VMEM_LIMIT)


def whole(shape):
    zeros = (0,) * len(shape)
    return pl.BlockSpec(shape, lambda *_: zeros, pipeline_mode=pl.Buffered(1))


def dot(a, b, dims=((1,), (0,))):
    return lax.dot_general(a, b, (dims, ((), ())), preferred_element_type=F32)


def one_hot(mask):
    return jnp.where(mask, 1.0, 0.0).astype(B16)


def slot_keys(ids_t, experts):
    toks = ids_t.shape[1]
    expert = iota((experts, toks), 0)
    hit = jnp.zeros((experts, toks), F32)
    for k in range(ids_t.shape[0]):
        hit += jnp.where(ids_t[k : k + 1, :] == expert, 1.0, 0.0)
    earlier = one_hot(iota((toks, toks), 0) < iota((toks, toks), 1))
    rank = dot(hit.astype(B16), earlier)
    return jnp.where(hit > 0.0, rank, -1.0).astype(jnp.int32)


def per_slot(value):
    experts, toks = value.shape
    return jnp.broadcast_to(value[:, None, :], (experts, MAIN, toks)).reshape(
        experts * MAIN, toks
    )


def send_tokens_kernel(ids_ref, tok_ref, out_ref, key_ref):
    j = pl.program_id(0)
    tiles = pl.num_programs(0) - 1
    width = out_ref.shape[1]
    experts = out_ref.shape[0] // MAIN

    @pl.when(j == 0)
    def _():
        key_ref[...] = per_slot(slot_keys(ids_ref[...], experts))

    slot = iota(key_ref.shape, 0) % MAIN

    @pl.when(j < tiles)
    def _():
        cols = pl.ds(pl.multiple_of(j * width, width), width)
        out_ref[...] = dot(one_hot(key_ref[...] == slot), tok_ref[:, cols]).astype(B16)

    @pl.when(j == tiles)
    def _():
        ninth = key_ref[...] == MAIN
        total = jnp.zeros(out_ref.shape, F32)
        for i in range(MAIN):
            total += dot(one_hot(ninth & (slot == i)), tok_ref[:, i * width : (i + 1) * width])
        out_ref[...] = total.astype(B16)


def send_tokens(ids_t, tokens, experts):
    toks, depth = tokens.shape
    width = depth // MAIN
    return pl.pallas_call(
        send_tokens_kernel,
        grid=(MAIN + 1,),
        in_specs=[whole(ids_t.shape), whole(tokens.shape)],
        out_specs=pl.BlockSpec((experts * MAIN, width), lambda j: (0, j)),
        out_shape=jax.ShapeDtypeStruct((experts * MAIN, depth + width), B16),
        scratch_shapes=[pltpu.VMEM((experts * MAIN, toks), jnp.int32)],
        compiler_params=params(),
        name="send_tokens",
    )(ids_t, tokens)


def send_grads_kernel(ids_ref, weight_ref, *refs):
    *part_refs, out_ref, cot_ref, key_ref, row_ref, rep_ref = refs
    j = pl.program_id(0)
    tiles = pl.num_programs(0) - 1
    width = out_ref.shape[1]
    experts = out_ref.shape[0] // MAIN
    slots, toks = key_ref.shape

    @pl.when(j == 0)
    def _():
        ids = ids_ref[...]
        key = per_slot(slot_keys(ids, experts))
        key_ref[...] = key
        expert = iota((experts, toks), 0)
        weight = jnp.zeros((experts, toks), F32)
        for k in range(ids.shape[0]):
            weight += jnp.where(ids[k : k + 1, :] == expert, weight_ref[k : k + 1, :], 0.0)
        weight = per_slot(weight)
        slot = iota((slots, toks), 0) % MAIN
        main = jnp.sum(jnp.where(key == slot, weight, 0.0), axis=1, keepdims=True)
        ninth = jnp.sum(jnp.where(key == MAIN, weight, 0.0), axis=1, keepdims=True)
        row_ref[...] = jnp.where(iota(row_ref.shape, 1) == 0, main, ninth)
        total = sum(part[...].astype(F32) for part in part_refs)
        cot = (total / SEQ_LEN).astype(B16)
        cot_ref[...] = cot
        spread = one_hot(iota((toks, cot.shape[0]), 0) // SEQ_LEN == iota((toks, cot.shape[0]), 1))
        rep_ref[...] = dot(spread, cot).astype(B16)

    slot = iota((slots, toks), 0) % MAIN

    @pl.when(j < tiles)
    def _():
        cols = pl.ds(pl.multiple_of(j * width, width), width)
        rows = dot(one_hot(key_ref[...] == slot), rep_ref[:, cols])
        out_ref[...] = (rows * row_ref[:, 0:1]).astype(B16)

    @pl.when(j == tiles)
    def _():
        ninth = key_ref[...] == MAIN
        total = jnp.zeros(out_ref.shape, F32)
        for i in range(MAIN):
            total += dot(one_hot(ninth & (slot == i)), rep_ref[:, i * width : (i + 1) * width])
        out_ref[...] = (total * row_ref[:, 1:2]).astype(B16)


def send_grads(ids_t, weights_t, parts, experts):
    toks = ids_t.shape[1]
    queries, depth = parts[0].shape
    width = depth // MAIN
    return pl.pallas_call(
        send_grads_kernel,
        grid=(MAIN + 1,),
        in_specs=[whole(ids_t.shape), whole(weights_t.shape)] + [whole(p.shape) for p in parts],
        out_specs=[
            pl.BlockSpec((experts * MAIN, width), lambda j: (0, j)),
            pl.BlockSpec((queries, depth), lambda j: (0, 0)),
        ],
        out_shape=[
            jax.ShapeDtypeStruct((experts * MAIN, depth + width), B16),
            jax.ShapeDtypeStruct((queries, depth), B16),
        ],
        scratch_shapes=[
            pltpu.VMEM((experts * MAIN, toks), jnp.int32),
            pltpu.VMEM((experts * MAIN, 128), F32),
            pltpu.VMEM((toks, depth), B16),
        ],
        compiler_params=params(),
        name="send_grads",
    )(ids_t, weights_t, *parts)


def unfold(fold, fold_ref, out_ref):
    sources, depth = out_ref.shape
    width = depth // MAIN
    for half in range(width // LANES):
        at = slice(half * LANES, (half + 1) * LANES)
        fold_ref[half] = fold[:, at].astype(F32)
        for i in range(MAIN):
            piece = fold_ref[half, pl.ds(i, sources, stride=MAIN), :]
            start = i * width + half * LANES
            out_ref[:, start : start + LANES] = piece.astype(B16)


def forward_kernel(x_ref, gate_ref, up_ref, hid_ref, cg_ref, cu_ref, x9_ref, fold_ref):
    j = pl.program_id(0)
    depth = gate_ref.shape[0]
    rows = x_ref.shape[0]

    @pl.when(j == 0)
    def _():
        unfold(x_ref[:, depth:], fold_ref, x9_ref)

    def finish(at, gate, up):
        sig = 1.0 / (1.0 + jnp.exp(-gate))
        act = gate * sig
        hid_ref[at, :] = (act * up).astype(B16)
        cg_ref[at, :] = (up * (sig * (1.0 + gate * (1.0 - sig)))).astype(B16)
        cu_ref[at, :] = act.astype(B16)

    step = rows // 4
    for m in range(4):
        x = x_ref[m * step : (m + 1) * step, :depth]
        finish(slice(m * step, (m + 1) * step), dot(x, gate_ref[...]), dot(x, up_ref[...]))
    x = x9_ref[...]
    finish(slice(rows, hid_ref.shape[0]), dot(x, gate_ref[...]), dot(x, up_ref[...]))


def forward(x, gate_up, hidden):
    rows, _ = x.shape
    depth = gate_up.shape[0]
    sources = rows // MAIN
    tile = 256
    tiles = hidden // tile
    col = lambda j: (0, j)
    part = pl.BlockSpec((rows + sources, tile), col)
    shape = jax.ShapeDtypeStruct((rows + sources, hidden), B16)
    return pl.pallas_call(
        forward_kernel,
        grid=(tiles,),
        in_specs=[
            whole(x.shape),
            pl.BlockSpec((depth, tile), col),
            pl.BlockSpec((depth, tile), lambda j: (0, j + tiles)),
        ],
        out_specs=[part, part, part, pl.BlockSpec((sources, depth), lambda j: (0, 0))],
        out_shape=[shape, shape, shape, jax.ShapeDtypeStruct((sources, depth), B16)],
        scratch_shapes=[pltpu.VMEM((depth // MAIN // LANES, rows, LANES), F32)],
        compiler_params=params(),
        cost_estimate=pl.CostEstimate(
            flops=2 * (rows + sources) * depth * 2 * hidden,
            bytes_accessed=2 * (x.size + gate_up.size + 3 * (rows + sources) * hidden),
            transcendentals=(rows + sources) * hidden,
        ),
        name="expert_forward",
    )(x, gate_up, gate_up)


def backward_kernel(
    first, g_ref, down_ref, cg_ref, cu_ref, w_ref, out_ref, pg_ref, g9_ref, fold_ref
):
    j = pl.program_id(0)
    rows = g_ref.shape[0]
    sources, depth = g9_ref.shape
    width = out_ref.shape[1]
    total = rows + sources
    tile = down_ref.shape[0]
    hidden = pg_ref.shape[1] // 2

    @pl.when(j == 0)
    def _():
        unfold(g_ref[:, depth:], fold_ref, g9_ref)

    @pl.when(j < first)
    def _():
        def finish(at, grad):
            gate_cols = pl.ds(pl.multiple_of(j * tile, tile), tile)
            up_cols = pl.ds(pl.multiple_of(hidden + j * tile, tile), tile)
            pg_ref[at, gate_cols] = (grad * cg_ref[at, :].astype(F32)).astype(B16)
            pg_ref[at, up_cols] = (grad * cu_ref[at, :].astype(F32)).astype(B16)

        step = rows // 4
        for m in range(4):
            at = slice(m * step, (m + 1) * step)
            finish(at, dot(g_ref[at, :depth], down_ref[...], ((1,), (1,))))
        finish(slice(rows, total), dot(g9_ref[...], down_ref[...], ((1,), (1,))))

    @pl.when((j >= first) & (j < first + MAIN))
    def _():
        step = rows // 4
        for m in range(4):
            at = slice(m * step, (m + 1) * step)
            out_ref[at, :] = dot(pg_ref[at, :], w_ref[...], ((1,), (1,))).astype(B16)
        ninth = dot(pg_ref[rows:total, :], w_ref[...], ((1,), (1,)))
        for half in range(width // LANES):
            fold_ref[half, pl.ds(j - first, sources, stride=MAIN), :] = ninth[
                :, half * LANES : (half + 1) * LANES
            ]

    @pl.when(j == first + MAIN)
    def _():
        for half in range(width // LANES):
            out_ref[:, half * LANES : (half + 1) * LANES] = fold_ref[half].astype(B16)


def backward(g, down, cg, cu, gate_up):
    rows, _ = g.shape
    hidden, depth = down.shape
    sources = rows // MAIN
    width = depth // MAIN
    tile = 256
    first = hidden // tile
    head = lambda j: (0, jnp.minimum(j, first - 1))
    part = pl.BlockSpec((rows + sources, tile), head)
    return pl.pallas_call(
        functools.partial(backward_kernel, first),
        grid=(first + MAIN + 1,),
        in_specs=[
            whole(g.shape),
            pl.BlockSpec((tile, depth), lambda j: (jnp.minimum(j, first - 1), 0)),
            part,
            part,
            pl.BlockSpec(
                (width, 2 * hidden), lambda j: (jnp.clip(j - first, 0, MAIN - 1), 0)
            ),
        ],
        out_specs=[
            pl.BlockSpec((rows, width), lambda j: (0, jnp.maximum(j - first, 0))),
            pl.BlockSpec((rows + sources, 2 * hidden), lambda j: (0, 0)),
            pl.BlockSpec((sources, depth), lambda j: (0, 0)),
        ],
        out_shape=[
            jax.ShapeDtypeStruct((rows, depth + width), B16),
            jax.ShapeDtypeStruct((rows + sources, 2 * hidden), B16),
            jax.ShapeDtypeStruct((sources, depth), B16),
        ],
        scratch_shapes=[pltpu.VMEM((width // LANES, rows, LANES), F32)],
        compiler_params=params(),
        cost_estimate=pl.CostEstimate(
            flops=6 * (rows + sources) * depth * hidden,
            bytes_accessed=2 * (2 * g.size + down.size + gate_up.size),
            transcendentals=0,
        ),
        name="expert_backward",
    )(g, down, cg, cu, gate_up)


def weight_grad_kernel(a_ref, a9_ref, b_ref, b9_ref, out_ref):
    rows = b_ref.shape[0]
    width = out_ref.shape[0]
    out_ref[...] = (
        dot(a_ref[:, :width], b_ref[...], ((0,), (0,))) + dot(a9_ref[...], b9_ref[...], ((0,), (0,)))
    ).astype(B16)


def weight_grad(a, a9, b, b9, columns, a9_block, b9_block, name):
    sources = a9.shape[0] if a9_block == 0 else a.shape[0] - 8 * (a.shape[0] // 9)
    rows = sources * MAIN
    width = a9.shape[1]
    tile = 256
    return pl.pallas_call(
        weight_grad_kernel,
        grid=(columns // tile,),
        in_specs=[
            pl.BlockSpec((rows, a.shape[1]), lambda j: (0, 0), pipeline_mode=pl.Buffered(1)),
            pl.BlockSpec(
                (sources, width), lambda j: (a9_block, 0), pipeline_mode=pl.Buffered(1)
            ),
            pl.BlockSpec((rows, tile), lambda j: (0, j)),
            pl.BlockSpec((sources, tile), lambda j: (b9_block, j)),
        ],
        out_specs=pl.BlockSpec((width, tile), lambda j: (0, j)),
        out_shape=jax.ShapeDtypeStruct((width, columns), B16),
        compiler_params=params(),
        cost_estimate=pl.CostEstimate(
            flops=2 * 9 * sources * width * columns,
            bytes_accessed=2 * (9 * sources * (width + columns) + width * columns),
            transcendentals=0,
        ),
        name=name,
    )(a, a9, b, b9)


def combine_kernel(ids_ref, cot_ref, got_ref, fold_ref, out_ref, key_ref):
    j = pl.program_id(0)
    toks, slots = key_ref.shape
    experts = slots // MAIN

    @pl.when(j == 0)
    def _():
        ids = ids_ref[...]
        expert = iota((toks, experts), 1)
        hit = jnp.zeros((toks, experts), F32)
        for k in range(ids.shape[1]):
            hit += jnp.where(ids[:, k : k + 1] == expert, 1.0, 0.0)
        earlier = one_hot(iota((toks, toks), 1) < iota((toks, toks), 0))
        rank = dot(earlier, hit.astype(B16))
        key = jnp.where(hit > 0.0, rank, -1.0).astype(B16)
        spread = one_hot(iota((experts, slots), 0) == iota((experts, slots), 1) // MAIN)
        key_ref[...] = dot(key, spread).astype(jnp.int32)

    key = key_ref[...]
    slot = iota(key.shape, 1) % MAIN
    queries = cot_ref.shape[0]
    spread = one_hot(iota((toks, queries), 0) // SEQ_LEN == iota((toks, queries), 1))
    total = dot(one_hot(key == slot), got_ref[...])
    total += dot(one_hot((key == MAIN) & (slot == j)), fold_ref[...])
    out_ref[...] = (dot(spread, cot_ref[...]) + total).astype(B16)


def combine(ids, cot, got):
    toks = ids.shape[0]
    queries, depth = cot.shape
    rows = got.shape[0]
    width = depth // MAIN
    return pl.pallas_call(
        combine_kernel,
        grid=(MAIN,),
        in_specs=[
            whole(ids.shape),
            pl.BlockSpec((queries, width), lambda j: (0, j)),
            pl.BlockSpec((rows, width), lambda j: (0, j)),
            pl.BlockSpec((rows, width), lambda j: (0, MAIN), pipeline_mode=pl.Buffered(1)),
        ],
        out_specs=pl.BlockSpec((toks, width), lambda j: (0, j)),
        out_shape=jax.ShapeDtypeStruct((toks, depth), B16),
        scratch_shapes=[pltpu.VMEM((toks, rows), jnp.int32)],
        compiler_params=params(),
        name="combine",
    )(ids, cot, got, got)


def scores_kernel(query_ref, passage_ref, score_ref, stat_ref):
    pieces, _, width = passage_ref.shape
    step = query_ref.shape[2]
    total = jnp.zeros(score_ref.shape, F32)
    for r in range(pieces):
        for h in range(width // step):
            part = passage_ref[r, :, h * step : (h + 1) * step]
            total += dot(part, query_ref[r * (width // step) + h], ((1,), (1,)))
    scores = total / SHARPNESS
    peak = jnp.max(scores, axis=0, keepdims=True)
    mass = jnp.sum(jnp.exp(scores - peak), axis=0, keepdims=True)
    score_ref[...] = scores
    stat_ref[...] = jnp.where(iota(stat_ref.shape, 0) == 0, peak, mass)


def local_scores(queries, passages):
    shape = (passages.shape[1], queries.shape[1])
    return pl.pallas_call(
        scores_kernel,
        out_shape=[
            jax.ShapeDtypeStruct(shape, F32),
            jax.ShapeDtypeStruct((8, shape[1]), F32),
        ],
        compiler_params=params(),
        name="local_scores",
    )(queries, passages)


def merged(stats):
    peak = functools.reduce(jnp.maximum, [s[0:1] for s in stats])
    mass = sum(s[1:2] * jnp.exp(s[0:1] - peak) for s in stats)
    return peak, mass


def query_part_kernel(at_ref, score_ref, pos_ref, passage_ref, *refs):
    count = len(refs) - 2
    side = count // 2
    stat_refs, out_refs = refs[:side], refs[side:count]
    dscore_ref, part_ref = refs[count], refs[count + 1]
    peak, mass = merged([s[...] for s in stat_refs])
    column = at_ref[1] + iota(score_ref.shape, 0)
    chosen = jnp.where(pos_ref[...] == column, 1.0, 0.0)
    soft = jnp.exp(score_ref[...] - peak) / mass
    dscore = ((soft - chosen) / SHARPNESS).astype(B16)
    dscore_ref[...] = dscore
    pieces, _, width = passage_ref.shape
    for r in range(pieces):
        part_ref[:, r * width : (r + 1) * width] = dot(
            dscore, passage_ref[r], ((0,), (0,))
        ).astype(B16)
    rows = out_refs[0].shape[0]
    for k in range(side):
        start = pl.multiple_of(((at_ref[0] + k) % side) * rows, rows)
        out_refs[k][...] = part_ref[pl.ds(start, rows), :]


def query_part(at, scores, positive, passages, stats):
    side = len(stats)
    pieces, _, width = passages.shape
    queries = scores.shape[1]
    depth = pieces * width
    smem = pl.BlockSpec(memory_space=pltpu.SMEM)
    vmem = pl.BlockSpec(memory_space=pltpu.VMEM)
    out = pl.pallas_call(
        query_part_kernel,
        in_specs=[smem] + [vmem] * (3 + side),
        out_specs=[vmem] * (side + 1),
        out_shape=[jax.ShapeDtypeStruct((queries // side, depth), B16)] * side
        + [jax.ShapeDtypeStruct(scores.shape, B16)],
        scratch_shapes=[pltpu.VMEM((queries, depth), B16)],
        compiler_params=params(),
        name="query_part",
    )(at, scores, positive, passages, *stats)
    return out[:side], out[side]


def forwarded_kernel(at_ref, *refs):
    side = (len(refs) - 1) // 2
    total_ref = refs[-1]
    total_ref[...] = sum(p[...].astype(F32) for p in refs[:side])
    rows = refs[side].shape[0]
    for k in range(side):
        start = pl.multiple_of(((at_ref[0] + k) % side) * rows, rows)
        refs[side + k][...] = total_ref[pl.ds(start, rows), :].astype(B16)


def forwarded(at, parts):
    side = len(parts)
    rows, depth = parts[0].shape
    vmem = pl.BlockSpec(memory_space=pltpu.VMEM)
    return pl.pallas_call(
        forwarded_kernel,
        in_specs=[pl.BlockSpec(memory_space=pltpu.SMEM)] + [vmem] * side,
        out_specs=[vmem] * side,
        out_shape=[jax.ShapeDtypeStruct((rows // side, depth), B16)] * side,
        scratch_shapes=[pltpu.VMEM((rows, depth), F32)],
        compiler_params=params(),
        name="forwarded",
    )(at, *parts)


def passage_part_kernel(at_ref, dscore_ref, query_ref, *refs):
    peers = len(refs) - 1
    out_refs, part_ref = refs[:peers], refs[peers]
    pieces, _, step = query_ref.shape
    for c in range(pieces):
        part_ref[:, c * step : (c + 1) * step] = dot(dscore_ref[...], query_ref[c]).astype(B16)
    width = out_refs[0].shape[1]
    for k in range(peers):
        start = pl.multiple_of(((at_ref[0] + k) % peers) * width, width)
        out_refs[k][...] = part_ref[:, pl.ds(start, width)]


def passage_part(at, dscore, queries, peers):
    pieces, _, step = queries.shape
    depth = pieces * step
    rows = dscore.shape[0]
    vmem = pl.BlockSpec(memory_space=pltpu.VMEM)
    return pl.pallas_call(
        passage_part_kernel,
        in_specs=[pl.BlockSpec(memory_space=pltpu.SMEM), vmem, vmem],
        out_specs=[vmem] * peers,
        out_shape=[jax.ShapeDtypeStruct((rows, depth // peers), B16)] * peers,
        scratch_shapes=[pltpu.VMEM((rows, depth), B16)],
        compiler_params=params(),
        name="passage_part",
    )(at, dscore, queries)


def sent_to_all(value, axis):
    peers = lax.axis_size(axis)
    return lax.all_to_all(
        jnp.broadcast_to(value[None], (peers, *value.shape)), axis, 0, 0, tiled=True
    )


def ring_steps(size, side, stride):
    def moved(i, k):
        at = i // stride % side
        return i + ((at + k) % side - at) * stride

    return [[(i, moved(i, k)) for i in range(size)] for k in range(1, side)]


def passed(values, axis, steps):
    return [values[0]] + [lax.ppermute(v, axis, p) for v, p in zip(values[1:], steps)]


def exchanged(block, experts):
    rows, width = block.shape
    got = lax.all_to_all(
        block.reshape(experts, rows // experts, width), ("row", "col"), 0, 0, tiled=True
    )
    return got.reshape(rows, width)


def shards(
    question_vectors,
    document_vectors,
    positive,
    tokens,
    expert_ids,
    route_weights,
    expert_gate_up,
    expert_down,
):
    row_size = lax.axis_size("row")
    col_size = lax.axis_size("col")
    experts = row_size * col_size
    gate_up, down = expert_gate_up[0], expert_down[0]
    hidden = down.shape[0]

    ids_t, weights_t = expert_ids.T, route_weights.T
    tokens_out = send_tokens(ids_t, tokens, experts)

    side = math.isqrt(col_size)
    far, near = ring_steps(col_size, side, side), ring_steps(col_size, side, 1)
    row, col = lax.axis_index("row"), lax.axis_index("col")
    passages = lax.all_gather(document_vectors, "row")
    queries = sent_to_all(question_vectors, "col")
    tokens_out, passages = lax.optimization_barrier((tokens_out, passages))
    scores, stat = local_scores(queries, passages)
    slot_inputs = exchanged(tokens_out, experts)
    stat = jnp.concatenate(merged(passed([stat] * side, "col", far)))
    stats = passed([stat] * side, "col", near)
    parts, dscore = query_part(
        jnp.stack([col // side, col * scores.shape[0]]), scores, positive[None], passages, stats
    )
    parts = forwarded((col % side)[None], passed(parts, "col", far))
    parts = passed(parts, "col", near)
    grads_out, cot = send_grads(ids_t, weights_t, parts, experts)
    slot_grads = exchanged(grads_out, experts)

    pieces = passage_part(row[None], dscore, queries, row_size)
    pieces = passed(pieces, "row", ring_steps(row_size, row_size, 1))
    passage_grad = sum(p.astype(F32) for p in pieces)

    hid, cg, cu, inputs9 = forward(slot_inputs, gate_up, hidden)
    back_out, pre_grad, grads9 = backward(slot_grads, down, cg, cu, gate_up)
    returned = exchanged(back_out, experts)
    down_grad = weight_grad(hid, hid, slot_grads, grads9, down.shape[1], MAIN, 0, "down_grad")
    gate_up_grad = weight_grad(
        slot_inputs, inputs9, pre_grad, pre_grad, 2 * hidden, 0, MAIN, "gate_up_grad"
    )
    token_grad = combine(expert_ids, cot, returned)
    return (passage_grad, token_grad, gate_up_grad[None], down_grad[None])


def solution(mesh):
    in_specs = (
        P("row", "col"),
        P("col", "row"),
        P("row"),
        P(("row", "col"), None),
        P(("row", "col"), None),
        P(("row", "col"), None),
        P(("row", "col"), None, None),
        P(("row", "col"), None, None),
    )
    out_specs = (
        P("col", "row"),
        P(("row", "col"), None),
        P(("row", "col"), None, None),
        P(("row", "col"), None, None),
    )
    return jax.shard_map(shards, mesh=mesh, in_specs=in_specs, out_specs=out_specs, check_vma=False)
```

```python
import functools

import jax
import jax.numpy as jnp
from jax import lax
from jax.experimental import pallas as pl
from jax.experimental.pallas import tpu as pltpu
from jax.sharding import PartitionSpec as P

SEQ_LEN = 8
SHARPNESS = 0.02
MAIN = 8
LANES = 128
B16 = jnp.bfloat16
F32 = jnp.float32
VMEM_LIMIT = 56 * 1024 * 1024


def iota(shape, dim):
    return lax.broadcasted_iota(jnp.int32, shape, dim)


def params():
    return pltpu.CompilerParams(vmem_limit_bytes=VMEM_LIMIT)


def whole(shape):
    zeros = (0,) * len(shape)
    return pl.BlockSpec(shape, lambda *_: zeros, pipeline_mode=pl.Buffered(1))


def dot(a, b, dims=((1,), (0,))):
    return lax.dot_general(a, b, (dims, ((), ())), preferred_element_type=F32)


def one_hot(mask):
    return jnp.where(mask, 1.0, 0.0).astype(B16)


def slot_keys(ids_t, experts):
    toks = ids_t.shape[1]
    expert = iota((experts, toks), 0)
    hit = jnp.zeros((experts, toks), F32)
    for k in range(ids_t.shape[0]):
        hit += jnp.where(ids_t[k : k + 1, :] == expert, 1.0, 0.0)
    earlier = one_hot(iota((toks, toks), 0) < iota((toks, toks), 1))
    rank = dot(hit.astype(B16), earlier)
    return jnp.where(hit > 0.0, rank, -1.0).astype(jnp.int32)


def per_slot(value):
    experts, toks = value.shape
    return jnp.broadcast_to(value[:, None, :], (experts, MAIN, toks)).reshape(
        experts * MAIN, toks
    )


def fold_up(ninth, fold_ref):
    experts, depth = ninth.shape
    width = depth // MAIN
    for half in range(width // LANES):
        for i in range(MAIN):
            start = i * width + half * LANES
            fold_ref[half, pl.ds(i, experts, stride=MAIN), :] = ninth[:, start : start + LANES]


def write_fold(fold_ref, out_ref):
    for half in range(fold_ref.shape[0]):
        out_ref[:, half * LANES : (half + 1) * LANES] = fold_ref[half].astype(B16)


def send_tokens_kernel(ids_ref, tok_ref, out_ref, mask_ref, fold_ref):
    j = pl.program_id(0)
    tiles = pl.num_programs(0) - 1
    width = out_ref.shape[1]
    experts = out_ref.shape[0] // MAIN

    @pl.when(j == 0)
    def _():
        key = slot_keys(ids_ref[...], experts)
        slot = iota(mask_ref.shape, 0) % MAIN
        mask_ref[...] = one_hot(per_slot(key) == slot)
        fold_up(dot(one_hot(key == MAIN), tok_ref[...]), fold_ref)

    @pl.when(j < tiles)
    def _():
        cols = pl.ds(pl.multiple_of(j * width, width), width)
        out_ref[...] = dot(mask_ref[...], tok_ref[:, cols]).astype(B16)

    @pl.when(j == tiles)
    def _():
        write_fold(fold_ref, out_ref)


def send_tokens(ids_t, tokens, experts):
    toks, depth = tokens.shape
    width = depth // MAIN
    rows = experts * MAIN
    return pl.pallas_call(
        send_tokens_kernel,
        grid=(MAIN + 1,),
        in_specs=[whole(ids_t.shape), whole(tokens.shape)],
        out_specs=pl.BlockSpec((rows, width), lambda j: (0, j)),
        out_shape=jax.ShapeDtypeStruct((rows, depth + width), B16),
        scratch_shapes=[
            pltpu.VMEM((rows, toks), B16),
            pltpu.VMEM((width // LANES, rows, LANES), F32),
        ],
        compiler_params=params(),
        name="send_tokens",
    )(ids_t, tokens)


def send_grads_kernel(
    ids_ref, weight_ref, part_ref, out_ref, cot_ref, mask_ref, row_ref, rep_ref, fold_ref
):
    j = pl.program_id(0)
    tiles = pl.num_programs(0) - 1
    width = out_ref.shape[1]
    experts = out_ref.shape[0] // MAIN
    slots, toks = mask_ref.shape

    @pl.when(j == 0)
    def _():
        ids = ids_ref[...]
        key = slot_keys(ids, experts)
        expert = iota((experts, toks), 0)
        weight = jnp.zeros((experts, toks), F32)
        for k in range(ids.shape[0]):
            weight += jnp.where(ids[k : k + 1, :] == expert, weight_ref[k : k + 1, :], 0.0)
        mine = per_slot(key) == iota((slots, toks), 0) % MAIN
        mask_ref[...] = one_hot(mine)
        row_ref[...] = jnp.sum(jnp.where(mine, per_slot(weight), 0.0), axis=1, keepdims=True)
        total = part_ref[0].astype(F32)
        for c in range(1, part_ref.shape[0]):
            total += part_ref[c].astype(F32)
        cot = (total / SEQ_LEN).astype(B16)
        cot_ref[...] = cot
        spread = one_hot(iota((toks, cot.shape[0]), 0) // SEQ_LEN == iota((toks, cot.shape[0]), 1))
        rep_ref[...] = dot(spread, cot).astype(B16)
        last = key == MAIN
        ninth = jnp.sum(jnp.where(last, weight, 0.0), axis=1, keepdims=True)
        fold_up(dot(one_hot(last), rep_ref[...]) * ninth, fold_ref)

    @pl.when(j < tiles)
    def _():
        cols = pl.ds(pl.multiple_of(j * width, width), width)
        out_ref[...] = (dot(mask_ref[...], rep_ref[:, cols]) * row_ref[...]).astype(B16)

    @pl.when(j == tiles)
    def _():
        write_fold(fold_ref, out_ref)


def send_grads(ids_t, weights_t, parts, experts):
    toks = ids_t.shape[1]
    _, queries, depth = parts.shape
    width = depth // MAIN
    rows = experts * MAIN
    return pl.pallas_call(
        send_grads_kernel,
        grid=(MAIN + 1,),
        in_specs=[whole(ids_t.shape), whole(weights_t.shape), whole(parts.shape)],
        out_specs=[
            pl.BlockSpec((rows, width), lambda j: (0, j)),
            pl.BlockSpec((queries, depth), lambda j: (0, 0)),
        ],
        out_shape=[
            jax.ShapeDtypeStruct((rows, depth + width), B16),
            jax.ShapeDtypeStruct((queries, depth), B16),
        ],
        scratch_shapes=[
            pltpu.VMEM((rows, toks), B16),
            pltpu.VMEM((rows, 1), F32),
            pltpu.VMEM((toks, depth), B16),
            pltpu.VMEM((width // LANES, rows, LANES), F32),
        ],
        compiler_params=params(),
        name="send_grads",
    )(ids_t, weights_t, parts)


def unfold(fold, fold_ref, out_ref):
    sources, depth = out_ref.shape
    width = depth // MAIN
    for half in range(width // LANES):
        at = slice(half * LANES, (half + 1) * LANES)
        fold_ref[half] = fold[:, at].astype(F32)
        for i in range(MAIN):
            piece = fold_ref[half, pl.ds(i, sources, stride=MAIN), :]
            start = i * width + half * LANES
            out_ref[:, start : start + LANES] = piece.astype(B16)


def forward_kernel(x_ref, gate_ref, up_ref, hid_ref, cg_ref, cu_ref, x9_ref, fold_ref):
    j = pl.program_id(0)
    depth = gate_ref.shape[0]
    rows = x_ref.shape[0]

    @pl.when(j == 0)
    def _():
        unfold(x_ref[:, depth:], fold_ref, x9_ref)

    def finish(at, gate, up):
        sig = 1.0 / (1.0 + jnp.exp(-gate))
        act = gate * sig
        hid_ref[at, :] = (act * up).astype(B16)
        cg_ref[at, :] = (up * (sig * (1.0 + gate * (1.0 - sig)))).astype(B16)
        cu_ref[at, :] = act.astype(B16)

    step = rows // 4
    for m in range(4):
        x = x_ref[m * step : (m + 1) * step, :depth]
        finish(slice(m * step, (m + 1) * step), dot(x, gate_ref[...]), dot(x, up_ref[...]))
    x = x9_ref[...]
    finish(slice(rows, hid_ref.shape[0]), dot(x, gate_ref[...]), dot(x, up_ref[...]))


def forward(x, gate_up, hidden):
    rows, _ = x.shape
    depth = gate_up.shape[0]
    sources = rows // MAIN
    tile = 256
    tiles = hidden // tile
    col = lambda j: (0, j)
    part = pl.BlockSpec((rows + sources, tile), col)
    shape = jax.ShapeDtypeStruct((rows + sources, hidden), B16)
    return pl.pallas_call(
        forward_kernel,
        grid=(tiles,),
        in_specs=[
            whole(x.shape),
            pl.BlockSpec((depth, tile), col),
            pl.BlockSpec((depth, tile), lambda j: (0, j + tiles)),
        ],
        out_specs=[part, part, part, pl.BlockSpec((sources, depth), lambda j: (0, 0))],
        out_shape=[shape, shape, shape, jax.ShapeDtypeStruct((sources, depth), B16)],
        scratch_shapes=[pltpu.VMEM((depth // MAIN // LANES, rows, LANES), F32)],
        compiler_params=params(),
        cost_estimate=pl.CostEstimate(
            flops=2 * (rows + sources) * depth * 2 * hidden,
            bytes_accessed=2 * (x.size + gate_up.size + 3 * (rows + sources) * hidden),
            transcendentals=(rows + sources) * hidden,
        ),
        name="expert_forward",
    )(x, gate_up, gate_up)


def backward_kernel(
    first, g_ref, down_ref, cg_ref, cu_ref, w_ref, out_ref, pg_ref, g9_ref, fold_ref
):
    j = pl.program_id(0)
    rows = g_ref.shape[0]
    sources, depth = g9_ref.shape
    width = out_ref.shape[1]
    total = rows + sources
    tile = down_ref.shape[0]
    hidden = pg_ref.shape[1] // 2

    @pl.when(j == 0)
    def _():
        unfold(g_ref[:, depth:], fold_ref, g9_ref)

    @pl.when(j < first)
    def _():
        def finish(at, grad):
            gate_cols = pl.ds(pl.multiple_of(j * tile, tile), tile)
            up_cols = pl.ds(pl.multiple_of(hidden + j * tile, tile), tile)
            pg_ref[at, gate_cols] = (grad * cg_ref[at, :].astype(F32)).astype(B16)
            pg_ref[at, up_cols] = (grad * cu_ref[at, :].astype(F32)).astype(B16)

        step = rows // 4
        for m in range(4):
            at = slice(m * step, (m + 1) * step)
            finish(at, dot(g_ref[at, :depth], down_ref[...], ((1,), (1,))))
        finish(slice(rows, total), dot(g9_ref[...], down_ref[...], ((1,), (1,))))

    @pl.when((j >= first) & (j < first + MAIN))
    def _():
        step = rows // 4
        for m in range(4):
            at = slice(m * step, (m + 1) * step)
            out_ref[at, :] = dot(pg_ref[at, :], w_ref[...], ((1,), (1,))).astype(B16)
        ninth = dot(pg_ref[rows:total, :], w_ref[...], ((1,), (1,)))
        for half in range(width // LANES):
            fold_ref[half, pl.ds(j - first, sources, stride=MAIN), :] = ninth[
                :, half * LANES : (half + 1) * LANES
            ]

    @pl.when(j == first + MAIN)
    def _():
        for half in range(width // LANES):
            out_ref[:, half * LANES : (half + 1) * LANES] = fold_ref[half].astype(B16)


def backward(g, down, cg, cu, gate_up):
    rows, _ = g.shape
    hidden, depth = down.shape
    sources = rows // MAIN
    width = depth // MAIN
    tile = 256
    first = hidden // tile
    head = lambda j: (0, jnp.minimum(j, first - 1))
    part = pl.BlockSpec((rows + sources, tile), head)
    return pl.pallas_call(
        functools.partial(backward_kernel, first),
        grid=(first + MAIN + 1,),
        in_specs=[
            whole(g.shape),
            pl.BlockSpec((tile, depth), lambda j: (jnp.minimum(j, first - 1), 0)),
            part,
            part,
            pl.BlockSpec(
                (width, 2 * hidden), lambda j: (jnp.clip(j - first, 0, MAIN - 1), 0)
            ),
        ],
        out_specs=[
            pl.BlockSpec((rows, width), lambda j: (0, jnp.maximum(j - first, 0))),
            pl.BlockSpec((rows + sources, 2 * hidden), lambda j: (0, 0)),
            pl.BlockSpec((sources, depth), lambda j: (0, 0)),
        ],
        out_shape=[
            jax.ShapeDtypeStruct((rows, depth + width), B16),
            jax.ShapeDtypeStruct((rows + sources, 2 * hidden), B16),
            jax.ShapeDtypeStruct((sources, depth), B16),
        ],
        scratch_shapes=[pltpu.VMEM((width // LANES, rows, LANES), F32)],
        compiler_params=params(),
        cost_estimate=pl.CostEstimate(
            flops=6 * (rows + sources) * depth * hidden,
            bytes_accessed=2 * (2 * g.size + down.size + gate_up.size),
            transcendentals=0,
        ),
        name="expert_backward",
    )(g, down, cg, cu, gate_up)


def weight_grad_kernel(a_ref, a9_ref, b_ref, b9_ref, out_ref):
    rows = b_ref.shape[0]
    width = out_ref.shape[0]
    out_ref[...] = (
        dot(a_ref[:, :width], b_ref[...], ((0,), (0,))) + dot(a9_ref[...], b9_ref[...], ((0,), (0,)))
    ).astype(B16)


def weight_grad(a, a9, b, b9, columns, a9_block, b9_block, name):
    sources = a9.shape[0] if a9_block == 0 else a.shape[0] - 8 * (a.shape[0] // 9)
    rows = sources * MAIN
    width = a9.shape[1]
    tile = 256
    return pl.pallas_call(
        weight_grad_kernel,
        grid=(columns // tile,),
        in_specs=[
            pl.BlockSpec((rows, a.shape[1]), lambda j: (0, 0), pipeline_mode=pl.Buffered(1)),
            pl.BlockSpec(
                (sources, width), lambda j: (a9_block, 0), pipeline_mode=pl.Buffered(1)
            ),
            pl.BlockSpec((rows, tile), lambda j: (0, j)),
            pl.BlockSpec((sources, tile), lambda j: (b9_block, j)),
        ],
        out_specs=pl.BlockSpec((width, tile), lambda j: (0, j)),
        out_shape=jax.ShapeDtypeStruct((width, columns), B16),
        compiler_params=params(),
        cost_estimate=pl.CostEstimate(
            flops=2 * 9 * sources * width * columns,
            bytes_accessed=2 * (9 * sources * (width + columns) + width * columns),
            transcendentals=0,
        ),
        name=name,
    )(a, a9, b, b9)


def combine_kernel(ids_ref, cot_ref, got_ref, fold_ref, out_ref, mask_ref, last_ref, ninth_ref, buf_ref):
    j = pl.program_id(0)
    toks, slots = mask_ref.shape
    experts = slots // MAIN
    width = out_ref.shape[1]

    @pl.when(j == 0)
    def _():
        ids = ids_ref[...]
        expert = iota((toks, experts), 1)
        hit = jnp.zeros((toks, experts), F32)
        for k in range(ids.shape[1]):
            hit += jnp.where(ids[:, k : k + 1] == expert, 1.0, 0.0)
        earlier = one_hot(iota((toks, toks), 1) < iota((toks, toks), 0))
        rank = dot(earlier, hit.astype(B16))
        key = jnp.where(hit > 0.0, rank, -1.0)
        last_ref[...] = one_hot(key == float(MAIN))
        spread = one_hot(iota((experts, slots), 0) == iota((experts, slots), 1) // MAIN)
        slot = (iota((toks, slots), 1) % MAIN).astype(F32)
        mask_ref[...] = one_hot(dot(key.astype(B16), spread) == slot)
        unfold(fold_ref[...], buf_ref, ninth_ref)

    queries = cot_ref.shape[0]
    spread = one_hot(iota((toks, queries), 0) // SEQ_LEN == iota((toks, queries), 1))
    cols = pl.ds(pl.multiple_of(j * width, width), width)
    total = dot(mask_ref[...], got_ref[...]) + dot(last_ref[...], ninth_ref[:, cols])
    out_ref[...] = (dot(spread, cot_ref[...]) + total).astype(B16)


def combine(ids, cot, got):
    toks = ids.shape[0]
    queries, depth = cot.shape
    rows = got.shape[0]
    experts = rows // MAIN
    fold = depth // MAIN
    width = 2 * fold
    return pl.pallas_call(
        combine_kernel,
        grid=(depth // width,),
        in_specs=[
            whole(ids.shape),
            pl.BlockSpec((queries, width), lambda j: (0, j)),
            pl.BlockSpec((rows, width), lambda j: (0, j)),
            pl.BlockSpec((rows, fold), lambda j: (0, MAIN), pipeline_mode=pl.Buffered(1)),
        ],
        out_specs=pl.BlockSpec((toks, width), lambda j: (0, j)),
        out_shape=jax.ShapeDtypeStruct((toks, depth), B16),
        scratch_shapes=[
            pltpu.VMEM((toks, rows), B16),
            pltpu.VMEM((toks, experts), B16),
            pltpu.VMEM((experts, depth), B16),
            pltpu.VMEM((fold // LANES, rows, LANES), F32),
        ],
        compiler_params=params(),
        name="combine",
    )(ids, cot, got, got)


def scores_kernel(query_ref, passage_ref, score_ref, stat_ref):
    pieces, _, width = passage_ref.shape
    step = query_ref.shape[2]
    total = jnp.zeros(score_ref.shape, F32)
    for r in range(pieces):
        for h in range(width // step):
            part = passage_ref[r, :, h * step : (h + 1) * step]
            total += dot(part, query_ref[r * (width // step) + h], ((1,), (1,)))
    scores = total / SHARPNESS
    peak = jnp.max(scores, axis=0, keepdims=True)
    mass = jnp.sum(jnp.exp(scores - peak), axis=0, keepdims=True)
    score_ref[...] = scores
    stat_ref[...] = jnp.where(iota(stat_ref.shape, 0) == 0, peak, mass)


def local_scores(queries, passages):
    shape = (passages.shape[1], queries.shape[1])
    return pl.pallas_call(
        scores_kernel,
        out_shape=[
            jax.ShapeDtypeStruct(shape, F32),
            jax.ShapeDtypeStruct((8, shape[1]), F32),
        ],
        compiler_params=params(),
        name="local_scores",
    )(queries, passages)


def query_part_kernel(at_ref, score_ref, stat_ref, pos_ref, passage_ref, out_ref, dscore_ref):
    parts = [stat_ref[c] for c in range(stat_ref.shape[0])]
    peak = functools.reduce(jnp.maximum, [p[0:1] for p in parts])
    mass = sum(p[1:2] * jnp.exp(p[0:1] - peak) for p in parts)
    column = at_ref[0] + iota(score_ref.shape, 0)
    chosen = jnp.where(pos_ref[...] == column, 1.0, 0.0)
    soft = jnp.exp(score_ref[...] - peak) / mass
    dscore = ((soft - chosen) / SHARPNESS).astype(B16)
    dscore_ref[...] = dscore
    pieces, _, width = passage_ref.shape
    for r in range(pieces):
        out_ref[:, r * width : (r + 1) * width] = dot(
            dscore, passage_ref[r], ((0,), (0,))
        ).astype(B16)


def query_part(at, scores, stats, positive, passages):
    pieces, _, width = passages.shape
    smem = pl.BlockSpec(memory_space=pltpu.SMEM)
    vmem = pl.BlockSpec(memory_space=pltpu.VMEM)
    return pl.pallas_call(
        query_part_kernel,
        in_specs=[smem] + [vmem] * 4,
        out_specs=[vmem] * 2,
        out_shape=[
            jax.ShapeDtypeStruct((scores.shape[1], pieces * width), B16),
            jax.ShapeDtypeStruct(scores.shape, B16),
        ],
        compiler_params=params(),
        name="query_part",
    )(at, scores, stats, positive, passages)


def passage_part_kernel(dscore_ref, query_ref, out_ref):
    peers, _, width = out_ref.shape
    pieces, _, step = query_ref.shape
    for c in range(pieces):
        at = c * step
        out_ref[at // width, :, at % width : at % width + step] = dot(
            dscore_ref[...], query_ref[c]
        ).astype(B16)


def passage_part(dscore, queries, peers):
    pieces, _, step = queries.shape
    vmem = pl.BlockSpec(memory_space=pltpu.VMEM)
    return pl.pallas_call(
        passage_part_kernel,
        in_specs=[vmem, vmem],
        out_specs=vmem,
        out_shape=jax.ShapeDtypeStruct((peers, dscore.shape[0], pieces * step // peers), B16),
        compiler_params=params(),
        name="passage_part",
    )(dscore, queries)


def sent_to_all(value, axis):
    peers = lax.axis_size(axis)
    return lax.all_to_all(
        jnp.broadcast_to(value[None], (peers, *value.shape)), axis, 0, 0, tiled=True
    )


def exchanged(block, experts):
    rows, width = block.shape
    got = lax.all_to_all(
        block.reshape(experts, rows // experts, width), ("row", "col"), 0, 0, tiled=True
    )
    return got.reshape(rows, width)


def shards(
    question_vectors,
    document_vectors,
    positive,
    tokens,
    expert_ids,
    route_weights,
    expert_gate_up,
    expert_down,
):
    row_size = lax.axis_size("row")
    col_size = lax.axis_size("col")
    experts = row_size * col_size
    gate_up, down = expert_gate_up[0], expert_down[0]
    hidden = down.shape[0]

    ids_t, weights_t = expert_ids.T, route_weights.T
    tokens_out = send_tokens(ids_t, tokens, experts)

    passages = lax.all_gather(document_vectors, "row")
    queries = sent_to_all(question_vectors, "col")
    scores, stat = local_scores(queries, passages)
    stats = sent_to_all(stat, "col")
    at = lax.axis_index("col") * scores.shape[0]
    part, dscore = query_part(at[None], scores, stats, positive[None], passages)
    parts = lax.all_to_all(
        part.reshape(col_size, -1, part.shape[1]), "col", 0, 0, tiled=True
    )
    slot_inputs = exchanged(tokens_out, experts)
    grads_out, cot = send_grads(ids_t, weights_t, parts, experts)
    pieces = passage_part(dscore, queries, row_size)
    grads_out, pieces = lax.optimization_barrier((grads_out, pieces))
    passage_sum = lax.psum_scatter(pieces, "row")
    slot_grads = exchanged(grads_out, experts)

    hid, cg, cu, inputs9 = forward(slot_inputs, gate_up, hidden)
    cg, passage_sum = lax.optimization_barrier((cg, passage_sum))
    passage_grad = passage_sum.astype(F32)
    back_out, pre_grad, grads9 = backward(slot_grads, down, cg, cu, gate_up)
    returned = exchanged(back_out, experts)
    down_grad = weight_grad(hid, hid, slot_grads, grads9, down.shape[1], MAIN, 0, "down_grad")
    gate_up_grad = weight_grad(
        slot_inputs, inputs9, pre_grad, pre_grad, 2 * hidden, 0, MAIN, "gate_up_grad"
    )
    token_grad = combine(expert_ids, cot, returned)
    return (passage_grad, token_grad, gate_up_grad[None], down_grad[None])


def solution(mesh):
    in_specs = (
        P("row", "col"),
        P("col", "row"),
        P("row"),
        P(("row", "col"), None),
        P(("row", "col"), None),
        P(("row", "col"), None),
        P(("row", "col"), None, None),
        P(("row", "col"), None, None),
    )
    out_specs = (
        P("col", "row"),
        P(("row", "col"), None),
        P(("row", "col"), None, None),
        P(("row", "col"), None, None),
    )
    return jax.shard_map(shards, mesh=mesh, in_specs=in_specs, out_specs=out_specs, check_vma=False)
```

```python
import functools

import jax
import jax.numpy as jnp
from jax import lax
from jax.experimental import pallas as pl
from jax.experimental.pallas import tpu as pltpu
from jax.sharding import PartitionSpec as P

SEQ_LEN = 8
SHARPNESS = 0.02
MAIN = 8
LANES = 128
B16 = jnp.bfloat16
F32 = jnp.float32


def iota(shape, dim):
    return lax.broadcasted_iota(jnp.int32, shape, dim)


def params(mib=56):
    return pltpu.CompilerParams(vmem_limit_bytes=mib * 1024 * 1024)


def whole(shape):
    zeros = (0,) * len(shape)
    return pl.BlockSpec(shape, lambda *_: zeros, pipeline_mode=pl.Buffered(1))


def dot(a, b, dims=((1,), (0,))):
    return lax.dot_general(a, b, (dims, ((), ())), preferred_element_type=F32)


def one_hot(mask):
    return jnp.where(mask, 1.0, 0.0).astype(B16)


def slot_keys(ids_t, experts):
    toks = ids_t.shape[1]
    expert = iota((experts, toks), 0)
    hit = jnp.zeros((experts, toks), F32)
    for k in range(ids_t.shape[0]):
        hit += jnp.where(ids_t[k : k + 1, :] == expert, 1.0, 0.0)
    earlier = one_hot(iota((toks, toks), 0) < iota((toks, toks), 1))
    rank = dot(hit.astype(B16), earlier)
    return jnp.where(hit > 0.0, rank, -1.0).astype(jnp.int32)


def per_slot(value):
    experts, toks = value.shape
    return jnp.broadcast_to(value[:, None, :], (experts, MAIN, toks)).reshape(
        experts * MAIN, toks
    )


def fold_up(ninth, fold_ref):
    experts, depth = ninth.shape
    width = depth // MAIN
    for half in range(width // LANES):
        for i in range(MAIN):
            start = i * width + half * LANES
            fold_ref[half, pl.ds(i, experts, stride=MAIN), :] = ninth[:, start : start + LANES]


def write_fold(fold_ref, out_ref):
    for half in range(fold_ref.shape[0]):
        out_ref[:, half * LANES : (half + 1) * LANES] = fold_ref[half].astype(B16)


def send_tokens_kernel(ids_ref, tok_ref, out_ref, mask_ref, fold_ref):
    j = pl.program_id(0)
    tiles = pl.num_programs(0) - 1
    width = out_ref.shape[1]
    experts = out_ref.shape[0] // MAIN

    @pl.when(j == 0)
    def _():
        key = slot_keys(ids_ref[...], experts)
        slot = iota(mask_ref.shape, 0) % MAIN
        mask_ref[...] = one_hot(per_slot(key) == slot)
        fold_up(dot(one_hot(key == MAIN), tok_ref[...]), fold_ref)

    @pl.when(j < tiles)
    def _():
        cols = pl.ds(pl.multiple_of(j * width, width), width)
        out_ref[...] = dot(mask_ref[...], tok_ref[:, cols]).astype(B16)

    @pl.when(j == tiles)
    def _():
        write_fold(fold_ref, out_ref)


def send_tokens(ids_t, tokens, experts):
    toks, depth = tokens.shape
    width = depth // MAIN
    rows = experts * MAIN
    return pl.pallas_call(
        send_tokens_kernel,
        grid=(MAIN + 1,),
        in_specs=[whole(ids_t.shape), whole(tokens.shape)],
        out_specs=pl.BlockSpec((rows, width), lambda j: (0, j)),
        out_shape=jax.ShapeDtypeStruct((rows, depth + width), B16),
        scratch_shapes=[
            pltpu.VMEM((rows, toks), B16),
            pltpu.VMEM((width // LANES, rows, LANES), F32),
        ],
        compiler_params=params(24),
        name="send_tokens",
    )(ids_t, tokens)


def send_grads_kernel(
    ids_ref, weight_ref, part_hbm, out_ref, cot_ref, mask_ref, row_ref, rep_ref, fold_ref, part_ref
):
    j = pl.program_id(0)
    tiles = pl.num_programs(0) - 1
    width = out_ref.shape[1]
    experts = out_ref.shape[0] // MAIN
    slots, toks = mask_ref.shape

    @pl.when(j == 0)
    def _():
        pltpu.sync_copy(part_hbm, part_ref)
        ids = ids_ref[...]
        key = slot_keys(ids, experts)
        expert = iota((experts, toks), 0)
        weight = jnp.zeros((experts, toks), F32)
        for k in range(ids.shape[0]):
            weight += jnp.where(ids[k : k + 1, :] == expert, weight_ref[k : k + 1, :], 0.0)
        mine = per_slot(key) == iota((slots, toks), 0) % MAIN
        mask_ref[...] = one_hot(mine)
        row_ref[...] = jnp.sum(jnp.where(mine, per_slot(weight), 0.0), axis=1, keepdims=True)
        total = part_ref[0].astype(F32)
        for c in range(1, part_ref.shape[0]):
            total += part_ref[c].astype(F32)
        cot = (total / SEQ_LEN).astype(B16)
        cot_ref[...] = cot
        spread = one_hot(iota((toks, cot.shape[0]), 0) // SEQ_LEN == iota((toks, cot.shape[0]), 1))
        rep_ref[...] = dot(spread, cot).astype(B16)
        last = key == MAIN
        ninth = jnp.sum(jnp.where(last, weight, 0.0), axis=1, keepdims=True)
        fold_up(dot(one_hot(last), rep_ref[...]) * ninth, fold_ref)

    @pl.when(j < tiles)
    def _():
        cols = pl.ds(pl.multiple_of(j * width, width), width)
        out_ref[...] = (dot(mask_ref[...], rep_ref[:, cols]) * row_ref[...]).astype(B16)

    @pl.when(j == tiles)
    def _():
        write_fold(fold_ref, out_ref)


def send_grads(ids_t, weights_t, parts, experts):
    toks = ids_t.shape[1]
    _, queries, depth = parts.shape
    width = depth // MAIN
    rows = experts * MAIN
    return pl.pallas_call(
        send_grads_kernel,
        grid=(MAIN + 1,),
        in_specs=[
            whole(ids_t.shape),
            whole(weights_t.shape),
            pl.BlockSpec(memory_space=pl.ANY),
        ],
        out_specs=[
            pl.BlockSpec((rows, width), lambda j: (0, j)),
            pl.BlockSpec((queries, depth), lambda j: (0, 0)),
        ],
        out_shape=[
            jax.ShapeDtypeStruct((rows, depth + width), B16),
            jax.ShapeDtypeStruct((queries, depth), B16),
        ],
        scratch_shapes=[
            pltpu.VMEM((rows, toks), B16),
            pltpu.VMEM((rows, 1), F32),
            pltpu.VMEM((toks, depth), B16),
            pltpu.VMEM((width // LANES, rows, LANES), F32),
            pltpu.VMEM(parts.shape, B16),
        ],
        compiler_params=params(24),
        name="send_grads",
    )(ids_t, weights_t, parts)


def unfold(fold, fold_ref, out_ref):
    sources, depth = out_ref.shape
    width = depth // MAIN
    for half in range(width // LANES):
        at = slice(half * LANES, (half + 1) * LANES)
        fold_ref[half] = fold[:, at].astype(F32)
        for i in range(MAIN):
            piece = fold_ref[half, pl.ds(i, sources, stride=MAIN), :]
            start = i * width + half * LANES
            out_ref[:, start : start + LANES] = piece.astype(B16)


def forward_kernel(x_ref, gate_ref, up_ref, hid_ref, cg_ref, cu_ref, x9_ref, fold_ref):
    j = pl.program_id(0)
    depth = gate_ref.shape[0]
    rows = x_ref.shape[0]

    @pl.when(j == 0)
    def _():
        unfold(x_ref[:, depth:], fold_ref, x9_ref)

    def finish(at, gate, up):
        sig = 1.0 / (1.0 + jnp.exp(-gate))
        act = gate * sig
        hid_ref[at, :] = (act * up).astype(B16)
        cg_ref[at, :] = (up * (sig * (1.0 + gate * (1.0 - sig)))).astype(B16)
        cu_ref[at, :] = act.astype(B16)

    step = rows // 4
    for m in range(4):
        x = x_ref[m * step : (m + 1) * step, :depth]
        finish(slice(m * step, (m + 1) * step), dot(x, gate_ref[...]), dot(x, up_ref[...]))
    x = x9_ref[...]
    finish(slice(rows, hid_ref.shape[0]), dot(x, gate_ref[...]), dot(x, up_ref[...]))


def forward(x, gate_up, hidden):
    rows, _ = x.shape
    depth = gate_up.shape[0]
    sources = rows // MAIN
    tile = 256
    tiles = hidden // tile
    col = lambda j: (0, j)
    part = pl.BlockSpec((rows + sources, tile), col)
    shape = jax.ShapeDtypeStruct((rows + sources, hidden), B16)
    return pl.pallas_call(
        forward_kernel,
        grid=(tiles,),
        in_specs=[
            whole(x.shape),
            pl.BlockSpec((depth, tile), col),
            pl.BlockSpec((depth, tile), lambda j: (0, j + tiles)),
        ],
        out_specs=[part, part, part, pl.BlockSpec((sources, depth), lambda j: (0, 0))],
        out_shape=[shape, shape, shape, jax.ShapeDtypeStruct((sources, depth), B16)],
        scratch_shapes=[pltpu.VMEM((depth // MAIN // LANES, rows, LANES), F32)],
        compiler_params=params(),
        cost_estimate=pl.CostEstimate(
            flops=2 * (rows + sources) * depth * 2 * hidden,
            bytes_accessed=2 * (x.size + gate_up.size + 3 * (rows + sources) * hidden),
            transcendentals=(rows + sources) * hidden,
        ),
        name="expert_forward",
    )(x, gate_up, gate_up)


def backward_kernel(
    first, g_ref, down_ref, cg_ref, cu_ref, w_ref, out_ref, pair_ref, g9_ref, pg_ref, fold_ref
):
    j = pl.program_id(0)
    rows = g_ref.shape[0]
    sources, depth = g9_ref.shape
    width = out_ref.shape[1]
    total = rows + sources
    tile = down_ref.shape[0]
    hidden = pg_ref.shape[1] // 2


    @pl.when(j == 0)
    def _():
        unfold(g_ref[:, depth:], fold_ref, g9_ref)

    @pl.when(j < first)
    def _():
        def finish(at, grad):
            gate_cols = pl.ds(pl.multiple_of(j * tile, tile), tile)
            up_cols = pl.ds(pl.multiple_of(hidden + j * tile, tile), tile)
            gate = (grad * cg_ref[at, :].astype(F32)).astype(B16)
            up = (grad * cu_ref[at, :].astype(F32)).astype(B16)
            pg_ref[at, gate_cols] = gate
            pg_ref[at, up_cols] = up
            pair_ref[at, :tile] = gate
            pair_ref[at, tile:] = up

        step = rows // 4
        for m in range(4):
            at = slice(m * step, (m + 1) * step)
            finish(at, dot(g_ref[at, :depth], down_ref[...], ((1,), (1,))))
        finish(slice(rows, total), dot(g9_ref[...], down_ref[...], ((1,), (1,))))

    @pl.when((j >= first) & (j < first + MAIN))
    def _():
        grads = dot(pg_ref[...], w_ref[...], ((1,), (1,)))
        out_ref[...] = grads[:rows].astype(B16)
        ninth = grads[rows:]
        for half in range(width // LANES):
            fold_ref[half, pl.ds(j - first, sources, stride=MAIN), :] = ninth[
                :, half * LANES : (half + 1) * LANES
            ]

    @pl.when(j == first + MAIN)
    def _():
        for half in range(width // LANES):
            out_ref[:, half * LANES : (half + 1) * LANES] = fold_ref[half].astype(B16)


def backward(g, down, cg, cu, gate_up):
    rows, _ = g.shape
    hidden, depth = down.shape
    sources = rows // MAIN
    width = depth // MAIN
    tile = 256
    first = hidden // tile
    head = lambda j: (0, jnp.minimum(j, first - 1))
    part = pl.BlockSpec((rows + sources, tile), head)
    return pl.pallas_call(
        functools.partial(backward_kernel, first),
        grid=(first + MAIN + 1,),
        in_specs=[
            whole(g.shape),
            pl.BlockSpec((tile, depth), lambda j: (jnp.minimum(j, first - 1), 0)),
            part,
            part,
            pl.BlockSpec(
                (width, 2 * hidden), lambda j: (jnp.clip(j - first, 0, MAIN - 1), 0)
            ),
        ],
        out_specs=[
            pl.BlockSpec((rows, width), lambda j: (0, jnp.maximum(j - first, 0))),
            pl.BlockSpec((rows + sources, 2 * tile), head),
            pl.BlockSpec((sources, depth), lambda j: (0, 0)),
        ],
        out_shape=[
            jax.ShapeDtypeStruct((rows, depth + width), B16),
            jax.ShapeDtypeStruct((rows + sources, 2 * hidden), B16),
            jax.ShapeDtypeStruct((sources, depth), B16),
        ],
        scratch_shapes=[
            pltpu.VMEM((rows + sources, 2 * hidden), B16),
            pltpu.VMEM((width // LANES, rows, LANES), F32),
        ],
        compiler_params=params(),
        cost_estimate=pl.CostEstimate(
            flops=6 * (rows + sources) * depth * hidden,
            bytes_accessed=2 * (2 * g.size + down.size + gate_up.size),
            transcendentals=0,
        ),
        name="expert_backward",
    )(g, down, cg, cu, gate_up)


def weight_grad_kernel(a_ref, a9_ref, b_ref, b9_ref, out_ref):
    rows = b_ref.shape[0]
    width = out_ref.shape[0]
    out_ref[...] = (
        dot(a_ref[:, :width], b_ref[...], ((0,), (0,))) + dot(a9_ref[...], b9_ref[...], ((0,), (0,)))
    ).astype(B16)


def weight_grad(a, a9, b, b9, columns, a9_block, b9_block, name, pairs=False):
    sources = a9.shape[0] if a9_block == 0 else a.shape[0] - 8 * (a.shape[0] // 9)
    rows = sources * MAIN
    width = a9.shape[1]
    tile = 256
    half = columns // tile // 2
    place = (lambda j: (0, j // 2 + (j % 2) * half)) if pairs else (lambda j: (0, j))
    return pl.pallas_call(
        weight_grad_kernel,
        grid=(columns // tile,),
        in_specs=[
            pl.BlockSpec((rows, a.shape[1]), lambda j: (0, 0), pipeline_mode=pl.Buffered(1)),
            pl.BlockSpec(
                (sources, width), lambda j: (a9_block, 0), pipeline_mode=pl.Buffered(1)
            ),
            pl.BlockSpec((rows, tile), lambda j: (0, j)),
            pl.BlockSpec((sources, tile), lambda j: (b9_block, j)),
        ],
        out_specs=pl.BlockSpec((width, tile), place),
        out_shape=jax.ShapeDtypeStruct((width, columns), B16),
        compiler_params=params(),
        cost_estimate=pl.CostEstimate(
            flops=2 * 9 * sources * width * columns,
            bytes_accessed=2 * (9 * sources * (width + columns) + width * columns),
            transcendentals=0,
        ),
        name=name,
    )(a, a9, b, b9)


def plan_kernel(ids_ref, mask_ref, last_ref):
    toks, slots = mask_ref.shape
    experts = slots // MAIN
    ids = ids_ref[...]
    expert = iota((toks, experts), 1)
    hit = jnp.zeros((toks, experts), F32)
    for k in range(ids.shape[1]):
        hit += jnp.where(ids[:, k : k + 1] == expert, 1.0, 0.0)
    earlier = one_hot(iota((toks, toks), 1) < iota((toks, toks), 0))
    rank = dot(earlier, hit.astype(B16))
    key = jnp.where(hit > 0.0, rank, -1.0)
    last_ref[...] = one_hot(key == float(MAIN))
    spread = one_hot(iota((experts, slots), 0) == iota((experts, slots), 1) // MAIN)
    slot = (iota((toks, slots), 1) % MAIN).astype(F32)
    mask_ref[...] = one_hot(dot(key.astype(B16), spread) == slot)


def combine_plan(ids, experts):
    toks = ids.shape[0]
    return pl.pallas_call(
        plan_kernel,
        out_shape=[
            jax.ShapeDtypeStruct((toks, experts * MAIN), B16),
            jax.ShapeDtypeStruct((toks, experts), B16),
        ],
        compiler_params=params(16),
        name="combine_plan",
    )(ids)


def combine_kernel(mask_ref, last_ref, cot_ref, got_ref, fold_ref, out_ref, ninth_ref, buf_ref):
    j = pl.program_id(0)
    toks = mask_ref.shape[0]
    width = out_ref.shape[1]

    @pl.when(j == 0)
    def _():
        unfold(fold_ref[...], buf_ref, ninth_ref)

    queries = cot_ref.shape[0]
    spread = one_hot(iota((toks, queries), 0) // SEQ_LEN == iota((toks, queries), 1))
    cols = pl.ds(pl.multiple_of(j * width, width), width)
    total = dot(mask_ref[...], got_ref[...]) + dot(last_ref[...], ninth_ref[:, cols])
    out_ref[...] = (dot(spread, cot_ref[...]) + total).astype(B16)


def combine(plan, cot, got):
    mask, last = plan
    toks, experts = last.shape
    queries, depth = cot.shape
    rows = got.shape[0]
    fold = depth // MAIN
    width = 2 * fold
    return pl.pallas_call(
        combine_kernel,
        grid=(depth // width,),
        in_specs=[
            whole(mask.shape),
            whole(last.shape),
            pl.BlockSpec((queries, width), lambda j: (0, j)),
            pl.BlockSpec((rows, width), lambda j: (0, j)),
            pl.BlockSpec((rows, fold), lambda j: (0, MAIN), pipeline_mode=pl.Buffered(1)),
        ],
        out_specs=pl.BlockSpec((toks, width), lambda j: (0, j)),
        out_shape=jax.ShapeDtypeStruct((toks, depth), B16),
        scratch_shapes=[
            pltpu.VMEM((experts, depth), B16),
            pltpu.VMEM((fold // LANES, rows, LANES), F32),
        ],
        compiler_params=params(32),
        name="combine",
    )(mask, last, cot, got, got)


def scores_kernel(query_hbm, passage_ref, score_ref, stat_ref, query_ref):
    pltpu.sync_copy(query_hbm, query_ref)
    pieces, _, width = passage_ref.shape
    step = query_ref.shape[2]
    total = jnp.zeros(score_ref.shape, F32)
    for r in range(pieces):
        for h in range(width // step):
            part = passage_ref[r, :, h * step : (h + 1) * step]
            total += dot(part, query_ref[r * (width // step) + h], ((1,), (1,)))
    scores = total / SHARPNESS
    peak = jnp.max(scores, axis=0, keepdims=True)
    mass = jnp.sum(jnp.exp(scores - peak), axis=0, keepdims=True)
    score_ref[...] = scores
    stat_ref[...] = jnp.where(iota(stat_ref.shape, 0) == 0, peak, mass)


def local_scores(queries, passages):
    shape = (passages.shape[1], queries.shape[1])
    return pl.pallas_call(
        scores_kernel,
        in_specs=[pl.BlockSpec(memory_space=pl.ANY), pl.BlockSpec(memory_space=pltpu.VMEM)],
        scratch_shapes=[pltpu.VMEM(queries.shape, B16)],
        out_shape=[
            jax.ShapeDtypeStruct(shape, F32),
            jax.ShapeDtypeStruct((2, shape[1]), F32),
        ],
        compiler_params=params(16),
        name="local_scores",
    )(queries, passages)


def query_part_kernel(
    at_ref, score_ref, stat_hbm, pos_ref, passage_ref, out_ref, dscore_ref, stat_ref
):
    pltpu.sync_copy(stat_hbm, stat_ref)
    parts = [stat_ref[c] for c in range(stat_ref.shape[0])]
    peak = functools.reduce(jnp.maximum, [p[0:1] for p in parts])
    mass = sum(p[1:2] * jnp.exp(p[0:1] - peak) for p in parts)
    column = at_ref[0] + iota(score_ref.shape, 0)
    chosen = jnp.where(pos_ref[...] == column, 1.0, 0.0)
    soft = jnp.exp(score_ref[...] - peak) / mass
    dscore = ((soft - chosen) / SHARPNESS).astype(B16)
    dscore_ref[...] = dscore
    pieces, _, width = passage_ref.shape
    for r in range(pieces):
        out_ref[:, r * width : (r + 1) * width] = dot(
            dscore, passage_ref[r], ((0,), (0,))
        ).astype(B16)


def query_part(at, scores, stats, positive, passages):
    pieces, _, width = passages.shape
    smem = pl.BlockSpec(memory_space=pltpu.SMEM)
    vmem = pl.BlockSpec(memory_space=pltpu.VMEM)
    return pl.pallas_call(
        query_part_kernel,
        in_specs=[smem, vmem, pl.BlockSpec(memory_space=pl.ANY), vmem, vmem],
        out_specs=[vmem] * 2,
        scratch_shapes=[pltpu.VMEM(stats.shape, F32)],
        out_shape=[
            jax.ShapeDtypeStruct((scores.shape[1], pieces * width), B16),
            jax.ShapeDtypeStruct(scores.shape, B16),
        ],
        compiler_params=params(16),
        name="query_part",
    )(at, scores, stats, positive, passages)


def passage_part_kernel(dscore_ref, query_hbm, out_ref, query_ref):
    pltpu.sync_copy(query_hbm, query_ref)
    peers, _, width = out_ref.shape
    pieces, _, step = query_ref.shape
    for c in range(pieces):
        at = c * step
        out_ref[at // width, :, at % width : at % width + step] = dot(
            dscore_ref[...], query_ref[c]
        ).astype(B16)


def passage_part(dscore, queries, peers):
    pieces, _, step = queries.shape
    vmem = pl.BlockSpec(memory_space=pltpu.VMEM)
    return pl.pallas_call(
        passage_part_kernel,
        in_specs=[vmem, pl.BlockSpec(memory_space=pl.ANY)],
        out_specs=vmem,
        scratch_shapes=[pltpu.VMEM(queries.shape, B16)],
        out_shape=jax.ShapeDtypeStruct((peers, dscore.shape[0], pieces * step // peers), B16),
        compiler_params=params(16),
        name="passage_part",
    )(dscore, queries)


def sent_to_all(value, axis):
    peers = lax.axis_size(axis)
    return lax.all_to_all(
        jnp.broadcast_to(value[None], (peers, *value.shape)), axis, 0, 0, tiled=True
    )


def exchanged(block, experts):
    rows, width = block.shape
    got = lax.all_to_all(
        block.reshape(experts, rows // experts, width), ("row", "col"), 0, 0, tiled=True
    )
    return got.reshape(rows, width)


def shards(
    question_vectors,
    document_vectors,
    positive,
    tokens,
    expert_ids,
    route_weights,
    expert_gate_up,
    expert_down,
):
    row_size = lax.axis_size("row")
    col_size = lax.axis_size("col")
    experts = row_size * col_size
    gate_up, down = expert_gate_up[0], expert_down[0]
    hidden = down.shape[0]

    ids_t, weights_t = expert_ids.T, route_weights.T
    tokens_out = send_tokens(ids_t, tokens, experts)

    passages = lax.all_gather(document_vectors, "row")
    queries = sent_to_all(question_vectors, "col")
    scores, stat = local_scores(queries, passages)
    stats = sent_to_all(stat, "col")
    at = lax.axis_index("col") * scores.shape[0]
    part, dscore = query_part(at[None], scores, stats, positive[None], passages)
    parts = lax.all_to_all(
        part.reshape(col_size, -1, part.shape[1]), "col", 0, 0, tiled=True
    )
    slot_inputs = exchanged(tokens_out, experts)
    grads_out, cot = send_grads(ids_t, weights_t, parts, experts)
    pieces = passage_part(dscore, queries, row_size)
    slot_grads = exchanged(grads_out, experts)

    plan = combine_plan(expert_ids, experts)
    hid, cg, cu, inputs9 = forward(slot_inputs, gate_up, hidden)
    pieces, cg, plan = lax.optimization_barrier((pieces, cg, plan))
    passage_parts = lax.all_to_all(pieces, "row", 0, 0, tiled=True)
    passage_grad = jnp.sum(passage_parts.astype(F32), axis=0)
    back_out, pre_grad, grads9 = backward(slot_grads, down, cg, cu, gate_up)
    returned = exchanged(back_out, experts)
    down_grad = weight_grad(hid, hid, slot_grads, grads9, down.shape[1], MAIN, 0, "down_grad")
    gate_up_grad = weight_grad(
        slot_inputs, inputs9, pre_grad, pre_grad, 2 * hidden, 0, MAIN, "gate_up_grad", True
    )
    token_grad = combine(plan, cot, returned)
    return (passage_grad, token_grad, gate_up_grad[None], down_grad[None])


def solution(mesh):
    in_specs = (
        P("row", "col"),
        P("col", "row"),
        P("row"),
        P(("row", "col"), None),
        P(("row", "col"), None),
        P(("row", "col"), None),
        P(("row", "col"), None, None),
        P(("row", "col"), None, None),
    )
    out_specs = (
        P("col", "row"),
        P(("row", "col"), None),
        P(("row", "col"), None, None),
        P(("row", "col"), None, None),
    )
    return jax.shard_map(shards, mesh=mesh, in_specs=in_specs, out_specs=out_specs, check_vma=False)
```

```python
import functools

import jax
import jax.numpy as jnp
from jax import lax
from jax.experimental import pallas as pl
from jax.experimental.pallas import tpu as pltpu
from jax.sharding import PartitionSpec as P

SEQ_LEN = 8
SHARPNESS = 0.02
MAIN = 8
LANES = 128
B16 = jnp.bfloat16
F32 = jnp.float32


def iota(shape, dim):
    return lax.broadcasted_iota(jnp.int32, shape, dim)


def params(mib=56):
    return pltpu.CompilerParams(vmem_limit_bytes=mib * 1024 * 1024)


def whole(shape):
    zeros = (0,) * len(shape)
    return pl.BlockSpec(shape, lambda *_: zeros, pipeline_mode=pl.Buffered(1))


def dot(a, b, dims=((1,), (0,))):
    return lax.dot_general(a, b, (dims, ((), ())), preferred_element_type=F32)


def one_hot(mask):
    return jnp.where(mask, 1.0, 0.0).astype(B16)


def slot_keys(ids_t, experts):
    toks = ids_t.shape[1]
    expert = iota((experts, toks), 0)
    hit = jnp.zeros((experts, toks), F32)
    for k in range(ids_t.shape[0]):
        hit += jnp.where(ids_t[k : k + 1, :] == expert, 1.0, 0.0)
    earlier = one_hot(iota((toks, toks), 0) < iota((toks, toks), 1))
    rank = dot(hit.astype(B16), earlier)
    return jnp.where(hit > 0.0, rank, -1.0).astype(jnp.int32)


def per_slot(value):
    experts, toks = value.shape
    return jnp.broadcast_to(value[:, None, :], (experts, MAIN, toks)).reshape(
        experts * MAIN, toks
    )


def fold_up(ninth, fold_ref):
    experts, depth = ninth.shape
    width = depth // MAIN
    for half in range(width // LANES):
        for i in range(MAIN):
            start = i * width + half * LANES
            fold_ref[half, pl.ds(i, experts, stride=MAIN), :] = ninth[:, start : start + LANES]


def write_fold(fold_ref, out_ref):
    for half in range(fold_ref.shape[0]):
        out_ref[:, half * LANES : (half + 1) * LANES] = fold_ref[half].astype(B16)


def send_tokens_kernel(ids_ref, tok_ref, out_ref, mask_ref, fold_ref):
    j = pl.program_id(0)
    tiles = pl.num_programs(0) - 1
    width = out_ref.shape[1]
    experts = out_ref.shape[0] // MAIN

    @pl.when(j == 0)
    def _():
        key = slot_keys(ids_ref[...], experts)
        slot = iota(mask_ref.shape, 0) % MAIN
        mask_ref[...] = one_hot(per_slot(key) == slot)
        fold_up(dot(one_hot(key == MAIN), tok_ref[...]), fold_ref)

    @pl.when(j < tiles)
    def _():
        cols = pl.ds(pl.multiple_of(j * width, width), width)
        out_ref[...] = dot(mask_ref[...], tok_ref[:, cols]).astype(B16)

    @pl.when(j == tiles)
    def _():
        write_fold(fold_ref, out_ref)


def send_tokens(ids_t, tokens, experts):
    toks, depth = tokens.shape
    width = depth // MAIN
    rows = experts * MAIN
    return pl.pallas_call(
        send_tokens_kernel,
        grid=(MAIN + 1,),
        in_specs=[whole(ids_t.shape), whole(tokens.shape)],
        out_specs=pl.BlockSpec((rows, width), lambda j: (0, j)),
        out_shape=jax.ShapeDtypeStruct((rows, depth + width), B16),
        scratch_shapes=[
            pltpu.VMEM((rows, toks), B16),
            pltpu.VMEM((width // LANES, rows, LANES), F32),
        ],
        compiler_params=params(24),
        name="send_tokens",
    )(ids_t, tokens)


def send_grads_kernel(
    ids_ref, weight_ref, part_hbm, out_ref, cot_ref, mask_ref, row_ref, rep_ref, fold_ref, part_ref
):
    j = pl.program_id(0)
    tiles = pl.num_programs(0) - 1
    width = out_ref.shape[1]
    experts = out_ref.shape[0] // MAIN
    slots, toks = mask_ref.shape

    @pl.when(j == 0)
    def _():
        pltpu.sync_copy(part_hbm, part_ref)
        ids = ids_ref[...]
        key = slot_keys(ids, experts)
        expert = iota((experts, toks), 0)
        weight = jnp.zeros((experts, toks), F32)
        for k in range(ids.shape[0]):
            weight += jnp.where(ids[k : k + 1, :] == expert, weight_ref[k : k + 1, :], 0.0)
        mine = per_slot(key) == iota((slots, toks), 0) % MAIN
        mask_ref[...] = one_hot(mine)
        row_ref[...] = jnp.sum(jnp.where(mine, per_slot(weight), 0.0), axis=1, keepdims=True)
        total = part_ref[0].astype(F32)
        for c in range(1, part_ref.shape[0]):
            total += part_ref[c].astype(F32)
        cot = (total / SEQ_LEN).astype(B16)
        cot_ref[...] = cot
        spread = one_hot(iota((toks, cot.shape[0]), 0) // SEQ_LEN == iota((toks, cot.shape[0]), 1))
        rep_ref[...] = dot(spread, cot).astype(B16)
        last = key == MAIN
        ninth = jnp.sum(jnp.where(last, weight, 0.0), axis=1, keepdims=True)
        fold_up(dot(one_hot(last), rep_ref[...]) * ninth, fold_ref)

    @pl.when(j < tiles)
    def _():
        cols = pl.ds(pl.multiple_of(j * width, width), width)
        out_ref[...] = (dot(mask_ref[...], rep_ref[:, cols]) * row_ref[...]).astype(B16)

    @pl.when(j == tiles)
    def _():
        write_fold(fold_ref, out_ref)


def send_grads(ids_t, weights_t, parts, experts):
    toks = ids_t.shape[1]
    _, queries, depth = parts.shape
    width = depth // MAIN
    rows = experts * MAIN
    return pl.pallas_call(
        send_grads_kernel,
        grid=(MAIN + 1,),
        in_specs=[
            whole(ids_t.shape),
            whole(weights_t.shape),
            pl.BlockSpec(memory_space=pl.ANY),
        ],
        out_specs=[
            pl.BlockSpec((rows, width), lambda j: (0, j)),
            pl.BlockSpec((queries, depth), lambda j: (0, 0)),
        ],
        out_shape=[
            jax.ShapeDtypeStruct((rows, depth + width), B16),
            jax.ShapeDtypeStruct((queries, depth), B16),
        ],
        scratch_shapes=[
            pltpu.VMEM((rows, toks), B16),
            pltpu.VMEM((rows, 1), F32),
            pltpu.VMEM((toks, depth), B16),
            pltpu.VMEM((width // LANES, rows, LANES), F32),
            pltpu.VMEM(parts.shape, B16),
        ],
        compiler_params=params(24),
        name="send_grads",
    )(ids_t, weights_t, parts)


def unfold(fold, fold_ref, out_ref):
    sources, depth = out_ref.shape
    width = depth // MAIN
    for half in range(width // LANES):
        at = slice(half * LANES, (half + 1) * LANES)
        fold_ref[half] = fold[:, at].astype(F32)
        for i in range(MAIN):
            piece = fold_ref[half, pl.ds(i, sources, stride=MAIN), :]
            start = i * width + half * LANES
            out_ref[:, start : start + LANES] = piece.astype(B16)


def forward_kernel(x_ref, gate_ref, up_ref, hid_ref, cg_ref, cu_ref, x9_ref, fold_ref):
    j = pl.program_id(0)
    depth = gate_ref.shape[0]
    rows = x_ref.shape[0]

    @pl.when(j == 0)
    def _():
        unfold(x_ref[:, depth:], fold_ref, x9_ref)

    def finish(at, gate, up):
        sig = 1.0 / (1.0 + jnp.exp(-gate))
        act = gate * sig
        hid_ref[at, :] = (act * up).astype(B16)
        cg_ref[at, :] = (up * (sig * (1.0 + gate * (1.0 - sig)))).astype(B16)
        cu_ref[at, :] = act.astype(B16)

    step = rows // 4
    for m in range(4):
        x = x_ref[m * step : (m + 1) * step, :depth]
        finish(slice(m * step, (m + 1) * step), dot(x, gate_ref[...]), dot(x, up_ref[...]))
    x = x9_ref[...]
    finish(slice(rows, hid_ref.shape[0]), dot(x, gate_ref[...]), dot(x, up_ref[...]))


def forward(x, gate_up, hidden):
    rows, _ = x.shape
    depth = gate_up.shape[0]
    sources = rows // MAIN
    tile = 256
    tiles = hidden // tile
    col = lambda j: (0, j)
    part = pl.BlockSpec((rows + sources, tile), col)
    shape = jax.ShapeDtypeStruct((rows + sources, hidden), B16)
    return pl.pallas_call(
        forward_kernel,
        grid=(tiles,),
        in_specs=[
            whole(x.shape),
            pl.BlockSpec((depth, tile), col),
            pl.BlockSpec((depth, tile), lambda j: (0, j + tiles)),
        ],
        out_specs=[part, part, part, pl.BlockSpec((sources, depth), lambda j: (0, 0))],
        out_shape=[shape, shape, shape, jax.ShapeDtypeStruct((sources, depth), B16)],
        scratch_shapes=[pltpu.VMEM((depth // MAIN // LANES, rows, LANES), F32)],
        compiler_params=params(),
        cost_estimate=pl.CostEstimate(
            flops=2 * (rows + sources) * depth * 2 * hidden,
            bytes_accessed=2 * (x.size + gate_up.size + 3 * (rows + sources) * hidden),
            transcendentals=(rows + sources) * hidden,
        ),
        name="expert_forward",
    )(x, gate_up, gate_up)


def backward_kernel(
    first, g_ref, down_ref, cg_ref, cu_ref, w_ref, out_ref, pair_ref, g9_ref, pg_ref, fold_ref
):
    j = pl.program_id(0)
    rows = g_ref.shape[0]
    sources, depth = g9_ref.shape
    width = out_ref.shape[1]
    total = rows + sources
    tile = down_ref.shape[0]
    hidden = pg_ref.shape[1] // 2


    @pl.when(j == 0)
    def _():
        unfold(g_ref[:, depth:], fold_ref, g9_ref)

    @pl.when(j < first)
    def _():
        def finish(at, grad):
            gate_cols = pl.ds(pl.multiple_of(j * tile, tile), tile)
            up_cols = pl.ds(pl.multiple_of(hidden + j * tile, tile), tile)
            gate = (grad * cg_ref[at, :].astype(F32)).astype(B16)
            up = (grad * cu_ref[at, :].astype(F32)).astype(B16)
            pg_ref[at, gate_cols] = gate
            pg_ref[at, up_cols] = up
            pair_ref[at, :tile] = gate
            pair_ref[at, tile:] = up

        step = rows // 4
        for m in range(4):
            at = slice(m * step, (m + 1) * step)
            finish(at, dot(g_ref[at, :depth], down_ref[...], ((1,), (1,))))
        finish(slice(rows, total), dot(g9_ref[...], down_ref[...], ((1,), (1,))))

    @pl.when((j >= first) & (j < first + MAIN))
    def _():
        grads = dot(pg_ref[...], w_ref[...], ((1,), (1,)))
        out_ref[...] = grads[:rows].astype(B16)
        ninth = grads[rows:]
        for half in range(width // LANES):
            fold_ref[half, pl.ds(j - first, sources, stride=MAIN), :] = ninth[
                :, half * LANES : (half + 1) * LANES
            ]

    @pl.when(j == first + MAIN)
    def _():
        for half in range(width // LANES):
            out_ref[:, half * LANES : (half + 1) * LANES] = fold_ref[half].astype(B16)


def backward(g, down, cg, cu, gate_up):
    rows, _ = g.shape
    hidden, depth = down.shape
    sources = rows // MAIN
    width = depth // MAIN
    tile = 256
    first = hidden // tile
    head = lambda j: (0, jnp.minimum(j, first - 1))
    part = pl.BlockSpec((rows + sources, tile), head)
    return pl.pallas_call(
        functools.partial(backward_kernel, first),
        grid=(first + MAIN + 1,),
        in_specs=[
            whole(g.shape),
            pl.BlockSpec((tile, depth), lambda j: (jnp.minimum(j, first - 1), 0)),
            part,
            part,
            pl.BlockSpec(
                (width, 2 * hidden), lambda j: (jnp.clip(j - first, 0, MAIN - 1), 0)
            ),
        ],
        out_specs=[
            pl.BlockSpec((rows, width), lambda j: (0, jnp.maximum(j - first, 0))),
            pl.BlockSpec((rows + sources, 2 * tile), head),
            pl.BlockSpec((sources, depth), lambda j: (0, 0)),
        ],
        out_shape=[
            jax.ShapeDtypeStruct((rows, depth + width), B16),
            jax.ShapeDtypeStruct((rows + sources, 2 * hidden), B16),
            jax.ShapeDtypeStruct((sources, depth), B16),
        ],
        scratch_shapes=[
            pltpu.VMEM((rows + sources, 2 * hidden), B16),
            pltpu.VMEM((width // LANES, rows, LANES), F32),
        ],
        compiler_params=params(),
        cost_estimate=pl.CostEstimate(
            flops=6 * (rows + sources) * depth * hidden,
            bytes_accessed=2 * (2 * g.size + down.size + gate_up.size),
            transcendentals=0,
        ),
        name="expert_backward",
    )(g, down, cg, cu, gate_up)


def weight_grad_kernel(a_ref, a9_ref, b_ref, b9_ref, out_ref):
    rows = b_ref.shape[0]
    width = out_ref.shape[0]
    out_ref[...] = (
        dot(a_ref[:, :width], b_ref[...], ((0,), (0,))) + dot(a9_ref[...], b9_ref[...], ((0,), (0,)))
    ).astype(B16)


def weight_grad(a, a9, b, b9, columns, a9_block, b9_block, name, pairs=False):
    sources = a9.shape[0] if a9_block == 0 else a.shape[0] - 8 * (a.shape[0] // 9)
    rows = sources * MAIN
    width = a9.shape[1]
    tile = 256
    half = columns // tile // 2
    place = (lambda j: (0, j // 2 + (j % 2) * half)) if pairs else (lambda j: (0, j))
    return pl.pallas_call(
        weight_grad_kernel,
        grid=(columns // tile,),
        in_specs=[
            pl.BlockSpec((rows, a.shape[1]), lambda j: (0, 0), pipeline_mode=pl.Buffered(1)),
            pl.BlockSpec(
                (sources, width), lambda j: (a9_block, 0), pipeline_mode=pl.Buffered(1)
            ),
            pl.BlockSpec((rows, tile), lambda j: (0, j)),
            pl.BlockSpec((sources, tile), lambda j: (b9_block, j)),
        ],
        out_specs=pl.BlockSpec((width, tile), place),
        out_shape=jax.ShapeDtypeStruct((width, columns), B16),
        compiler_params=params(),
        cost_estimate=pl.CostEstimate(
            flops=2 * 9 * sources * width * columns,
            bytes_accessed=2 * (9 * sources * (width + columns) + width * columns),
            transcendentals=0,
        ),
        name=name,
    )(a, a9, b, b9)


def plan_kernel(ids_ref, mask_ref, last_ref):
    toks, slots = mask_ref.shape
    experts = slots // MAIN
    ids = ids_ref[...]
    expert = iota((toks, experts), 1)
    hit = jnp.zeros((toks, experts), F32)
    for k in range(ids.shape[1]):
        hit += jnp.where(ids[:, k : k + 1] == expert, 1.0, 0.0)
    earlier = one_hot(iota((toks, toks), 1) < iota((toks, toks), 0))
    rank = dot(earlier, hit.astype(B16))
    key = jnp.where(hit > 0.0, rank, -1.0)
    last_ref[...] = one_hot(key == float(MAIN))
    spread = one_hot(iota((experts, slots), 0) == iota((experts, slots), 1) // MAIN)
    slot = (iota((toks, slots), 1) % MAIN).astype(F32)
    mask_ref[...] = one_hot(dot(key.astype(B16), spread) == slot)


def combine_plan(ids, experts):
    toks = ids.shape[0]
    return pl.pallas_call(
        plan_kernel,
        out_shape=[
            jax.ShapeDtypeStruct((toks, experts * MAIN), B16),
            jax.ShapeDtypeStruct((toks, experts), B16),
        ],
        compiler_params=params(16),
        name="combine_plan",
    )(ids)


def combine_kernel(mask_ref, last_ref, cot_ref, got_ref, fold_ref, out_ref, ninth_ref, buf_ref):
    j = pl.program_id(0)
    toks = mask_ref.shape[0]
    width = out_ref.shape[1]

    @pl.when(j == 0)
    def _():
        unfold(fold_ref[...], buf_ref, ninth_ref)

    queries = cot_ref.shape[0]
    spread = one_hot(iota((toks, queries), 0) // SEQ_LEN == iota((toks, queries), 1))
    cols = pl.ds(pl.multiple_of(j * width, width), width)
    total = dot(mask_ref[...], got_ref[...]) + dot(last_ref[...], ninth_ref[:, cols])
    out_ref[...] = (dot(spread, cot_ref[...]) + total).astype(B16)


def combine(plan, cot, got):
    mask, last = plan
    toks, experts = last.shape
    queries, depth = cot.shape
    rows = got.shape[0]
    fold = depth // MAIN
    width = 2 * fold
    return pl.pallas_call(
        combine_kernel,
        grid=(depth // width,),
        in_specs=[
            whole(mask.shape),
            whole(last.shape),
            pl.BlockSpec((queries, width), lambda j: (0, j)),
            pl.BlockSpec((rows, width), lambda j: (0, j)),
            pl.BlockSpec((rows, fold), lambda j: (0, MAIN), pipeline_mode=pl.Buffered(1)),
        ],
        out_specs=pl.BlockSpec((toks, width), lambda j: (0, j)),
        out_shape=jax.ShapeDtypeStruct((toks, depth), B16),
        scratch_shapes=[
            pltpu.VMEM((experts, depth), B16),
            pltpu.VMEM((fold // LANES, rows, LANES), F32),
        ],
        compiler_params=params(32),
        name="combine",
    )(mask, last, cot, got, got)


def scores_kernel(query_hbm, passage_ref, score_ref, stat_ref, query_ref):
    pltpu.sync_copy(query_hbm, query_ref)
    pieces, _, width = passage_ref.shape
    step = query_ref.shape[2]
    total = jnp.zeros(score_ref.shape, F32)
    for r in range(pieces):
        for h in range(width // step):
            part = passage_ref[r, :, h * step : (h + 1) * step]
            total += dot(part, query_ref[r * (width // step) + h], ((1,), (1,)))
    scores = total / SHARPNESS
    peak = jnp.max(scores, axis=0, keepdims=True)
    mass = jnp.sum(jnp.exp(scores - peak), axis=0, keepdims=True)
    score_ref[...] = scores
    stat_ref[...] = jnp.where(iota(stat_ref.shape, 0) == 0, peak, mass)


def local_scores(queries, passages):
    shape = (passages.shape[1], queries.shape[1])
    return pl.pallas_call(
        scores_kernel,
        in_specs=[pl.BlockSpec(memory_space=pl.ANY), pl.BlockSpec(memory_space=pltpu.VMEM)],
        scratch_shapes=[pltpu.VMEM(queries.shape, B16)],
        out_shape=[
            jax.ShapeDtypeStruct(shape, F32),
            jax.ShapeDtypeStruct((2, shape[1]), F32),
        ],
        compiler_params=params(16),
        name="local_scores",
    )(queries, passages)


def query_part_kernel(
    at_ref, score_ref, stat_hbm, pos_ref, passage_ref, out_ref, dscore_ref, stat_ref
):
    pltpu.sync_copy(stat_hbm, stat_ref)
    parts = [stat_ref[c] for c in range(stat_ref.shape[0])]
    peak = functools.reduce(jnp.maximum, [p[0:1] for p in parts])
    mass = sum(p[1:2] * jnp.exp(p[0:1] - peak) for p in parts)
    column = at_ref[0] + iota(score_ref.shape, 0)
    chosen = jnp.where(pos_ref[...] == column, 1.0, 0.0)
    soft = jnp.exp(score_ref[...] - peak) / mass
    dscore = ((soft - chosen) / SHARPNESS).astype(B16)
    dscore_ref[...] = dscore
    pieces, _, width = passage_ref.shape
    for r in range(pieces):
        out_ref[:, r * width : (r + 1) * width] = dot(
            dscore, passage_ref[r], ((0,), (0,))
        ).astype(B16)


def query_part(at, scores, stats, positive, passages):
    pieces, _, width = passages.shape
    smem = pl.BlockSpec(memory_space=pltpu.SMEM)
    vmem = pl.BlockSpec(memory_space=pltpu.VMEM)
    return pl.pallas_call(
        query_part_kernel,
        in_specs=[smem, vmem, pl.BlockSpec(memory_space=pl.ANY), vmem, vmem],
        out_specs=[vmem] * 2,
        scratch_shapes=[pltpu.VMEM(stats.shape, F32)],
        out_shape=[
            jax.ShapeDtypeStruct((scores.shape[1], pieces * width), B16),
            jax.ShapeDtypeStruct(scores.shape, B16),
        ],
        compiler_params=params(16),
        name="query_part",
    )(at, scores, stats, positive, passages)


CORES = 2


def passage_part_kernel(at_ref, dscore_ref, query_hbm, own_ref, other_ref, query_ref, part_ref):
    pltpu.sync_copy(query_hbm, query_ref)
    chips, _, width = own_ref.shape
    pieces, _, step = query_ref.shape
    for c in range(pieces):
        at = c * step
        part_ref[at // width, :, at % width : at % width + step] = dot(
            dscore_ref[...], query_ref[c]
        ).astype(B16)
    core = at_ref[0] % CORES
    for y in range(chips):
        own_ref[y] = part_ref[y * CORES + core]
        other_ref[y] = part_ref[y * CORES + 1 - core]


def passage_part(at, dscore, queries, peers):
    pieces, _, step = queries.shape
    width = pieces * step // peers
    smem = pl.BlockSpec(memory_space=pltpu.SMEM)
    vmem = pl.BlockSpec(memory_space=pltpu.VMEM)
    half = jax.ShapeDtypeStruct((peers // CORES, dscore.shape[0], width), B16)
    return pl.pallas_call(
        passage_part_kernel,
        in_specs=[smem, vmem, pl.BlockSpec(memory_space=pl.ANY)],
        out_specs=[vmem, vmem],
        out_shape=[half, half],
        scratch_shapes=[
            pltpu.VMEM(queries.shape, B16),
            pltpu.VMEM((peers, dscore.shape[0], width), B16),
        ],
        compiler_params=params(16),
        name="passage_part",
    )(at, dscore, queries)


def pair_sum_kernel(at_ref, own_ref, got_ref, mine_ref, *out_refs):
    chips = own_ref.shape[0]
    chip = at_ref[0] // CORES

    def pair(k):
        y = (chip + k) % chips
        return own_ref[y].astype(F32) + got_ref[y].astype(F32)

    mine_ref[...] = pair(0)
    for k in range(1, chips):
        out_refs[k - 1][...] = pair(k).astype(B16)


def pair_sum(at, own, got):
    chips, rows, width = own.shape
    vmem = pl.BlockSpec(memory_space=pltpu.VMEM)
    return pl.pallas_call(
        pair_sum_kernel,
        in_specs=[pl.BlockSpec(memory_space=pltpu.SMEM), vmem, vmem],
        out_specs=[vmem] * chips,
        out_shape=[jax.ShapeDtypeStruct((rows, width), F32)]
        + [jax.ShapeDtypeStruct((rows, width), B16)] * (chips - 1),
        compiler_params=params(16),
        name="pair_sum",
    )(at, own, got)


def sent_to_all(value, axis):
    peers = lax.axis_size(axis)
    return lax.all_to_all(
        jnp.broadcast_to(value[None], (peers, *value.shape)), axis, 0, 0, tiled=True
    )


def exchanged(block, experts):
    rows, width = block.shape
    got = lax.all_to_all(
        block.reshape(experts, rows // experts, width), ("row", "col"), 0, 0, tiled=True
    )
    return got.reshape(rows, width)


def shards(
    question_vectors,
    document_vectors,
    positive,
    tokens,
    expert_ids,
    route_weights,
    expert_gate_up,
    expert_down,
):
    row_size = lax.axis_size("row")
    col_size = lax.axis_size("col")
    experts = row_size * col_size
    gate_up, down = expert_gate_up[0], expert_down[0]
    hidden = down.shape[0]

    ids_t, weights_t = expert_ids.T, route_weights.T
    tokens_out = send_tokens(ids_t, tokens, experts)

    passages = lax.all_gather(document_vectors, "row")
    queries = sent_to_all(question_vectors, "col")
    scores, stat = local_scores(queries, passages)
    stats = sent_to_all(stat, "col")
    at = lax.axis_index("col") * scores.shape[0]
    stats, tokens_out = lax.optimization_barrier((stats, tokens_out))
    part, dscore = query_part(at[None], scores, stats, positive[None], passages)
    parts = lax.all_to_all(
        part.reshape(col_size, -1, part.shape[1]), "col", 0, 0, tiled=True
    )
    row = lax.axis_index("row")[None]
    own, other = passage_part(row, dscore, queries, row_size)
    got = lax.ppermute(other, "row", [(i, i ^ 1) for i in range(row_size)])
    mine, *further = pair_sum(row, own, got)
    further = [
        lax.ppermute(
            value, "row", [(i, (i + k * CORES) % row_size) for i in range(row_size)]
        )
        for k, value in enumerate(further, 1)
    ]
    tokens_out, *further = lax.optimization_barrier((tokens_out, *further))
    passage_grad = mine + sum(value.astype(F32) for value in further)
    slot_inputs = exchanged(tokens_out, experts)
    grads_out, cot = send_grads(ids_t, weights_t, parts, experts)
    slot_grads = exchanged(grads_out, experts)

    plan = combine_plan(expert_ids, experts)
    hid, cg, cu, inputs9 = forward(slot_inputs, gate_up, hidden)
    passage_grad, cg, plan = lax.optimization_barrier((passage_grad, cg, plan))
    back_out, pre_grad, grads9 = backward(slot_grads, down, cg, cu, gate_up)
    returned = exchanged(back_out, experts)
    down_grad = weight_grad(hid, hid, slot_grads, grads9, down.shape[1], MAIN, 0, "down_grad")
    gate_up_grad = weight_grad(
        slot_inputs, inputs9, pre_grad, pre_grad, 2 * hidden, 0, MAIN, "gate_up_grad", True
    )
    token_grad = combine(plan, cot, returned)
    return (passage_grad, token_grad, gate_up_grad[None], down_grad[None])


def solution(mesh):
    in_specs = (
        P("row", "col"),
        P("col", "row"),
        P("row"),
        P(("row", "col"), None),
        P(("row", "col"), None),
        P(("row", "col"), None),
        P(("row", "col"), None, None),
        P(("row", "col"), None, None),
    )
    out_specs = (
        P("col", "row"),
        P(("row", "col"), None),
        P(("row", "col"), None, None),
        P(("row", "col"), None, None),
    )
    return jax.shard_map(shards, mesh=mesh, in_specs=in_specs, out_specs=out_specs, check_vma=False)
```

```python
import functools

import jax
import jax.numpy as jnp
from jax import lax
from jax.experimental import pallas as pl
from jax.experimental.pallas import tpu as pltpu
from jax.sharding import PartitionSpec as P

SEQ_LEN = 8
SHARPNESS = 0.02
MAIN = 8
LANES = 128
B16 = jnp.bfloat16
F32 = jnp.float32


def iota(shape, dim):
    return lax.broadcasted_iota(jnp.int32, shape, dim)


def params(mib=56):
    return pltpu.CompilerParams(vmem_limit_bytes=mib * 1024 * 1024)


def whole(shape):
    zeros = (0,) * len(shape)
    return pl.BlockSpec(shape, lambda *_: zeros, pipeline_mode=pl.Buffered(1))


def dot(a, b, dims=((1,), (0,))):
    return lax.dot_general(a, b, (dims, ((), ())), preferred_element_type=F32)


def one_hot(mask):
    return jnp.where(mask, 1.0, 0.0).astype(B16)


def slot_keys(ids_t, experts):
    toks = ids_t.shape[1]
    expert = iota((experts, toks), 0)
    hit = jnp.zeros((experts, toks), F32)
    for k in range(ids_t.shape[0]):
        hit += jnp.where(ids_t[k : k + 1, :] == expert, 1.0, 0.0)
    earlier = one_hot(iota((toks, toks), 0) < iota((toks, toks), 1))
    rank = dot(hit.astype(B16), earlier)
    return jnp.where(hit > 0.0, rank, -1.0).astype(jnp.int32)


def per_slot(value):
    experts, toks = value.shape
    return jnp.broadcast_to(value[:, None, :], (experts, MAIN, toks)).reshape(
        experts * MAIN, toks
    )


def fold_up(ninth, fold_ref):
    experts, depth = ninth.shape
    width = depth // MAIN
    for half in range(width // LANES):
        for i in range(MAIN):
            start = i * width + half * LANES
            fold_ref[half, pl.ds(i, experts, stride=MAIN), :] = ninth[:, start : start + LANES]


def write_fold(fold_ref, out_ref):
    for half in range(fold_ref.shape[0]):
        out_ref[:, half * LANES : (half + 1) * LANES] = fold_ref[half].astype(B16)


def send_tokens_kernel(ids_ref, tok_ref, out_ref, mask_ref, fold_ref):
    j = pl.program_id(0)
    tiles = pl.num_programs(0) - 1
    width = out_ref.shape[1]
    experts = out_ref.shape[0] // MAIN

    @pl.when(j == 0)
    def _():
        key = slot_keys(ids_ref[...], experts)
        slot = iota(mask_ref.shape, 0) % MAIN
        mask_ref[...] = one_hot(per_slot(key) == slot)
        fold_up(dot(one_hot(key == MAIN), tok_ref[...]), fold_ref)

    @pl.when(j < tiles)
    def _():
        cols = pl.ds(pl.multiple_of(j * width, width), width)
        out_ref[...] = dot(mask_ref[...], tok_ref[:, cols]).astype(B16)

    @pl.when(j == tiles)
    def _():
        write_fold(fold_ref, out_ref)


def send_tokens(ids_t, tokens, experts):
    toks, depth = tokens.shape
    width = depth // MAIN
    rows = experts * MAIN
    return pl.pallas_call(
        send_tokens_kernel,
        grid=(MAIN + 1,),
        in_specs=[whole(ids_t.shape), whole(tokens.shape)],
        out_specs=pl.BlockSpec((rows, width), lambda j: (0, j)),
        out_shape=jax.ShapeDtypeStruct((rows, depth + width), B16),
        scratch_shapes=[
            pltpu.VMEM((rows, toks), B16),
            pltpu.VMEM((width // LANES, rows, LANES), F32),
        ],
        compiler_params=params(24),
        name="send_tokens",
    )(ids_t, tokens)


def send_grads_kernel(
    ids_ref, weight_ref, part_hbm, out_ref, cot_ref, mask_ref, row_ref, rep_ref, fold_ref, part_ref
):
    j = pl.program_id(0)
    tiles = pl.num_programs(0) - 1
    width = out_ref.shape[1]
    experts = out_ref.shape[0] // MAIN
    slots, toks = mask_ref.shape

    @pl.when(j == 0)
    def _():
        pltpu.sync_copy(part_hbm, part_ref)
        ids = ids_ref[...]
        key = slot_keys(ids, experts)
        expert = iota((experts, toks), 0)
        weight = jnp.zeros((experts, toks), F32)
        for k in range(ids.shape[0]):
            weight += jnp.where(ids[k : k + 1, :] == expert, weight_ref[k : k + 1, :], 0.0)
        mine = per_slot(key) == iota((slots, toks), 0) % MAIN
        mask_ref[...] = one_hot(mine)
        row_ref[...] = jnp.sum(jnp.where(mine, per_slot(weight), 0.0), axis=1, keepdims=True)
        total = part_ref[0].astype(F32)
        for c in range(1, part_ref.shape[0]):
            total += part_ref[c].astype(F32)
        cot = (total / SEQ_LEN).astype(B16)
        cot_ref[...] = cot
        spread = one_hot(iota((toks, cot.shape[0]), 0) // SEQ_LEN == iota((toks, cot.shape[0]), 1))
        rep_ref[...] = dot(spread, cot).astype(B16)
        last = key == MAIN
        ninth = jnp.sum(jnp.where(last, weight, 0.0), axis=1, keepdims=True)
        fold_up(dot(one_hot(last), rep_ref[...]) * ninth, fold_ref)

    @pl.when(j < tiles)
    def _():
        cols = pl.ds(pl.multiple_of(j * width, width), width)
        out_ref[...] = (dot(mask_ref[...], rep_ref[:, cols]) * row_ref[...]).astype(B16)

    @pl.when(j == tiles)
    def _():
        write_fold(fold_ref, out_ref)


def send_grads(ids_t, weights_t, parts, experts):
    toks = ids_t.shape[1]
    _, queries, depth = parts.shape
    width = depth // MAIN
    rows = experts * MAIN
    return pl.pallas_call(
        send_grads_kernel,
        grid=(MAIN + 1,),
        in_specs=[
            whole(ids_t.shape),
            whole(weights_t.shape),
            pl.BlockSpec(memory_space=pl.ANY),
        ],
        out_specs=[
            pl.BlockSpec((rows, width), lambda j: (0, j)),
            pl.BlockSpec((queries, depth), lambda j: (0, 0)),
        ],
        out_shape=[
            jax.ShapeDtypeStruct((rows, depth + width), B16),
            jax.ShapeDtypeStruct((queries, depth), B16),
        ],
        scratch_shapes=[
            pltpu.VMEM((rows, toks), B16),
            pltpu.VMEM((rows, 1), F32),
            pltpu.VMEM((toks, depth), B16),
            pltpu.VMEM((width // LANES, rows, LANES), F32),
            pltpu.VMEM(parts.shape, B16),
        ],
        compiler_params=params(24),
        name="send_grads",
    )(ids_t, weights_t, parts)


def unfold(fold, fold_ref, out_ref):
    sources, depth = out_ref.shape
    width = depth // MAIN
    for half in range(width // LANES):
        at = slice(half * LANES, (half + 1) * LANES)
        fold_ref[half] = fold[:, at].astype(F32)
        for i in range(MAIN):
            piece = fold_ref[half, pl.ds(i, sources, stride=MAIN), :]
            start = i * width + half * LANES
            out_ref[:, start : start + LANES] = piece.astype(B16)


def forward_kernel(x_ref, gate_ref, up_ref, hid_ref, cg_ref, cu_ref, x9_ref, fold_ref):
    j = pl.program_id(0)
    depth = gate_ref.shape[0]
    rows = x_ref.shape[0]

    @pl.when(j == 0)
    def _():
        unfold(x_ref[:, depth:], fold_ref, x9_ref)

    def finish(at, gate, up):
        sig = 1.0 / (1.0 + jnp.exp(-gate))
        act = gate * sig
        hid_ref[at, :] = (act * up).astype(B16)
        cg_ref[at, :] = (up * (sig * (1.0 + gate * (1.0 - sig)))).astype(B16)
        cu_ref[at, :] = act.astype(B16)

    step = rows // 4
    for m in range(4):
        x = x_ref[m * step : (m + 1) * step, :depth]
        finish(slice(m * step, (m + 1) * step), dot(x, gate_ref[...]), dot(x, up_ref[...]))
    x = x9_ref[...]
    finish(slice(rows, hid_ref.shape[0]), dot(x, gate_ref[...]), dot(x, up_ref[...]))


def forward(x, gate_up, hidden):
    rows, _ = x.shape
    depth = gate_up.shape[0]
    sources = rows // MAIN
    tile = 256
    tiles = hidden // tile
    col = lambda j: (0, j)
    part = pl.BlockSpec((rows + sources, tile), col)
    shape = jax.ShapeDtypeStruct((rows + sources, hidden), B16)
    return pl.pallas_call(
        forward_kernel,
        grid=(tiles,),
        in_specs=[
            whole(x.shape),
            pl.BlockSpec((depth, tile), col),
            pl.BlockSpec((depth, tile), lambda j: (0, j + tiles)),
        ],
        out_specs=[part, part, part, pl.BlockSpec((sources, depth), lambda j: (0, 0))],
        out_shape=[shape, shape, shape, jax.ShapeDtypeStruct((sources, depth), B16)],
        scratch_shapes=[pltpu.VMEM((depth // MAIN // LANES, rows, LANES), F32)],
        compiler_params=params(),
        cost_estimate=pl.CostEstimate(
            flops=2 * (rows + sources) * depth * 2 * hidden,
            bytes_accessed=2 * (x.size + gate_up.size + 3 * (rows + sources) * hidden),
            transcendentals=(rows + sources) * hidden,
        ),
        name="expert_forward",
    )(x, gate_up, gate_up)


CHUNKS = 4


def backward_kernel(
    first, *refs
):
    g_refs, refs = refs[:CHUNKS], refs[CHUNKS:]
    down_ref, cg_ref, cu_ref, w_ref, out_ref, pair_ref, g9_ref, pg_ref, fold_ref = refs
    j = pl.program_id(0)
    step = g_refs[0].shape[0]
    rows = step * CHUNKS
    sources, depth = g9_ref.shape
    width = out_ref.shape[1]
    total = rows + sources
    tile = down_ref.shape[0]
    hidden = pg_ref.shape[1] // 2


    @pl.when(j == 0)
    def _():
        unfold(jnp.concatenate([g[:, depth:] for g in g_refs]), fold_ref, g9_ref)

    @pl.when(j < first)
    def _():
        def finish(at, grad):
            gate_cols = pl.ds(pl.multiple_of(j * tile, tile), tile)
            up_cols = pl.ds(pl.multiple_of(hidden + j * tile, tile), tile)
            gate = (grad * cg_ref[at, :].astype(F32)).astype(B16)
            up = (grad * cu_ref[at, :].astype(F32)).astype(B16)
            pg_ref[at, gate_cols] = gate
            pg_ref[at, up_cols] = up
            pair_ref[at, :tile] = gate
            pair_ref[at, tile:] = up

        for m in range(CHUNKS):
            at = slice(m * step, (m + 1) * step)
            finish(at, dot(g_refs[m][:, :depth], down_ref[...], ((1,), (1,))))
        finish(slice(rows, total), dot(g9_ref[...], down_ref[...], ((1,), (1,))))

    @pl.when((j >= first) & (j < first + MAIN))
    def _():
        grads = dot(pg_ref[...], w_ref[...], ((1,), (1,)))
        out_ref[...] = grads[:rows].astype(B16)
        ninth = grads[rows:]
        for half in range(width // LANES):
            fold_ref[half, pl.ds(j - first, sources, stride=MAIN), :] = ninth[
                :, half * LANES : (half + 1) * LANES
            ]

    @pl.when(j == first + MAIN)
    def _():
        for half in range(width // LANES):
            out_ref[:, half * LANES : (half + 1) * LANES] = fold_ref[half].astype(B16)


def backward(g, down, cg, cu, gate_up):
    rows, _ = g.shape
    hidden, depth = down.shape
    sources = rows // MAIN
    width = depth // MAIN
    tile = 256
    first = hidden // tile
    head = lambda j: (0, jnp.minimum(j, first - 1))
    part = pl.BlockSpec((rows + sources, tile), head)
    return pl.pallas_call(
        functools.partial(backward_kernel, first),
        grid=(first + MAIN + 1,),
        in_specs=[
            *[
                pl.BlockSpec(
                    (rows // CHUNKS, g.shape[1]),
                    lambda j, m=m: (m, 0),
                    pipeline_mode=pl.Buffered(1),
                )
                for m in range(CHUNKS)
            ],
            pl.BlockSpec((tile, depth), lambda j: (jnp.minimum(j, first - 1), 0)),
            part,
            part,
            pl.BlockSpec(
                (width, 2 * hidden), lambda j: (jnp.clip(j - first, 0, MAIN - 1), 0)
            ),
        ],
        out_specs=[
            pl.BlockSpec((rows, width), lambda j: (0, jnp.maximum(j - first, 0))),
            pl.BlockSpec((rows + sources, 2 * tile), head),
            pl.BlockSpec((sources, depth), lambda j: (0, 0)),
        ],
        out_shape=[
            jax.ShapeDtypeStruct((rows, depth + width), B16),
            jax.ShapeDtypeStruct((rows + sources, 2 * hidden), B16),
            jax.ShapeDtypeStruct((sources, depth), B16),
        ],
        scratch_shapes=[
            pltpu.VMEM((rows + sources, 2 * hidden), B16),
            pltpu.VMEM((width // LANES, rows, LANES), F32),
        ],
        compiler_params=params(),
        cost_estimate=pl.CostEstimate(
            flops=6 * (rows + sources) * depth * hidden,
            bytes_accessed=2 * (2 * g.size + down.size + gate_up.size),
            transcendentals=0,
        ),
        name="expert_backward",
    )(*[g] * CHUNKS, down, cg, cu, gate_up)


def weight_grad_kernel(a_ref, a9_ref, b_ref, b9_ref, out_ref):
    rows = b_ref.shape[0]
    width = out_ref.shape[0]
    out_ref[...] = (
        dot(a_ref[:, :width], b_ref[...], ((0,), (0,))) + dot(a9_ref[...], b9_ref[...], ((0,), (0,)))
    ).astype(B16)


def weight_grad(a, a9, b, b9, columns, a9_block, b9_block, name, pairs=False):
    sources = a9.shape[0] if a9_block == 0 else a.shape[0] - 8 * (a.shape[0] // 9)
    rows = sources * MAIN
    width = a9.shape[1]
    tile = 256
    half = columns // tile // 2
    place = (lambda j: (0, j // 2 + (j % 2) * half)) if pairs else (lambda j: (0, j))
    return pl.pallas_call(
        weight_grad_kernel,
        grid=(columns // tile,),
        in_specs=[
            pl.BlockSpec((rows, a.shape[1]), lambda j: (0, 0), pipeline_mode=pl.Buffered(1)),
            pl.BlockSpec(
                (sources, width), lambda j: (a9_block, 0), pipeline_mode=pl.Buffered(1)
            ),
            pl.BlockSpec((rows, tile), lambda j: (0, j)),
            pl.BlockSpec((sources, tile), lambda j: (b9_block, j)),
        ],
        out_specs=pl.BlockSpec((width, tile), place),
        out_shape=jax.ShapeDtypeStruct((width, columns), B16),
        compiler_params=params(),
        cost_estimate=pl.CostEstimate(
            flops=2 * 9 * sources * width * columns,
            bytes_accessed=2 * (9 * sources * (width + columns) + width * columns),
            transcendentals=0,
        ),
        name=name,
    )(a, a9, b, b9)


def plan_kernel(ids_ref, mask_ref, last_ref):
    toks, slots = mask_ref.shape
    experts = slots // MAIN
    ids = ids_ref[...]
    expert = iota((toks, experts), 1)
    hit = jnp.zeros((toks, experts), F32)
    for k in range(ids.shape[1]):
        hit += jnp.where(ids[:, k : k + 1] == expert, 1.0, 0.0)
    earlier = one_hot(iota((toks, toks), 1) < iota((toks, toks), 0))
    rank = dot(earlier, hit.astype(B16))
    key = jnp.where(hit > 0.0, rank, -1.0)
    last_ref[...] = one_hot(key == float(MAIN))
    spread = one_hot(iota((experts, slots), 0) == iota((experts, slots), 1) // MAIN)
    slot = (iota((toks, slots), 1) % MAIN).astype(F32)
    mask_ref[...] = one_hot(dot(key.astype(B16), spread) == slot)


def combine_plan(ids, experts):
    toks = ids.shape[0]
    return pl.pallas_call(
        plan_kernel,
        out_shape=[
            jax.ShapeDtypeStruct((toks, experts * MAIN), B16),
            jax.ShapeDtypeStruct((toks, experts), B16),
        ],
        compiler_params=params(16),
        name="combine_plan",
    )(ids)


def combine_kernel(mask_ref, last_ref, cot_ref, got_ref, fold_ref, out_ref, ninth_ref, buf_ref):
    j = pl.program_id(0)
    toks = mask_ref.shape[0]
    width = out_ref.shape[1]

    @pl.when(j == 0)
    def _():
        unfold(fold_ref[...], buf_ref, ninth_ref)

    queries = cot_ref.shape[0]
    spread = one_hot(iota((toks, queries), 0) // SEQ_LEN == iota((toks, queries), 1))
    cols = pl.ds(pl.multiple_of(j * width, width), width)
    total = dot(mask_ref[...], got_ref[...]) + dot(last_ref[...], ninth_ref[:, cols])
    out_ref[...] = (dot(spread, cot_ref[...]) + total).astype(B16)


def combine(plan, cot, got):
    mask, last = plan
    toks, experts = last.shape
    queries, depth = cot.shape
    rows = got.shape[0]
    fold = depth // MAIN
    width = 4 * fold
    return pl.pallas_call(
        combine_kernel,
        grid=(depth // width,),
        in_specs=[
            whole(mask.shape),
            whole(last.shape),
            pl.BlockSpec((queries, width), lambda j: (0, j)),
            pl.BlockSpec((rows, width), lambda j: (0, j)),
            pl.BlockSpec((rows, fold), lambda j: (0, MAIN), pipeline_mode=pl.Buffered(1)),
        ],
        out_specs=pl.BlockSpec((toks, width), lambda j: (0, j)),
        out_shape=jax.ShapeDtypeStruct((toks, depth), B16),
        scratch_shapes=[
            pltpu.VMEM((experts, depth), B16),
            pltpu.VMEM((fold // LANES, rows, LANES), F32),
        ],
        compiler_params=params(32),
        name="combine",
    )(mask, last, cot, got, got)


def scores_kernel(query_hbm, passage_ref, score_ref, stat_ref, query_ref):
    pltpu.sync_copy(query_hbm, query_ref)
    pieces, _, width = passage_ref.shape
    step = query_ref.shape[2]
    total = jnp.zeros(score_ref.shape, F32)
    for r in range(pieces):
        for h in range(width // step):
            part = passage_ref[r, :, h * step : (h + 1) * step]
            total += dot(part, query_ref[r * (width // step) + h], ((1,), (1,)))
    scores = total / SHARPNESS
    peak = jnp.max(scores, axis=0, keepdims=True)
    mass = jnp.sum(jnp.exp(scores - peak), axis=0, keepdims=True)
    score_ref[...] = scores
    stat_ref[...] = jnp.where(iota(stat_ref.shape, 0) == 0, peak, mass)


def local_scores(queries, passages):
    shape = (passages.shape[1], queries.shape[1])
    return pl.pallas_call(
        scores_kernel,
        in_specs=[pl.BlockSpec(memory_space=pl.ANY), pl.BlockSpec(memory_space=pltpu.VMEM)],
        scratch_shapes=[pltpu.VMEM(queries.shape, B16)],
        out_shape=[
            jax.ShapeDtypeStruct(shape, F32),
            jax.ShapeDtypeStruct((2, shape[1]), F32),
        ],
        compiler_params=params(16),
        name="local_scores",
    )(queries, passages)


def query_part_kernel(
    at_ref, score_ref, stat_hbm, pos_ref, passage_ref, out_ref, dscore_ref, stat_ref
):
    pltpu.sync_copy(stat_hbm, stat_ref)
    parts = [stat_ref[c] for c in range(stat_ref.shape[0])]
    peak = functools.reduce(jnp.maximum, [p[0:1] for p in parts])
    mass = sum(p[1:2] * jnp.exp(p[0:1] - peak) for p in parts)
    column = at_ref[0] + iota(score_ref.shape, 0)
    chosen = jnp.where(pos_ref[...] == column, 1.0, 0.0)
    soft = jnp.exp(score_ref[...] - peak) / mass
    dscore = ((soft - chosen) / SHARPNESS).astype(B16)
    dscore_ref[...] = dscore
    pieces, _, width = passage_ref.shape
    for r in range(pieces):
        out_ref[:, r * width : (r + 1) * width] = dot(
            dscore, passage_ref[r], ((0,), (0,))
        ).astype(B16)


def query_part(at, scores, stats, positive, passages):
    pieces, _, width = passages.shape
    smem = pl.BlockSpec(memory_space=pltpu.SMEM)
    vmem = pl.BlockSpec(memory_space=pltpu.VMEM)
    return pl.pallas_call(
        query_part_kernel,
        in_specs=[smem, vmem, pl.BlockSpec(memory_space=pl.ANY), vmem, vmem],
        out_specs=[vmem] * 2,
        scratch_shapes=[pltpu.VMEM(stats.shape, F32)],
        out_shape=[
            jax.ShapeDtypeStruct((scores.shape[1], pieces * width), B16),
            jax.ShapeDtypeStruct(scores.shape, B16),
        ],
        compiler_params=params(16),
        name="query_part",
    )(at, scores, stats, positive, passages)


CORES = 2


def passage_part_kernel(at_ref, dscore_ref, query_hbm, own_ref, other_ref, query_ref, part_ref):
    pltpu.sync_copy(query_hbm, query_ref)
    chips, _, width = own_ref.shape
    pieces, _, step = query_ref.shape
    for c in range(pieces):
        at = c * step
        part_ref[at // width, :, at % width : at % width + step] = dot(
            dscore_ref[...], query_ref[c]
        ).astype(B16)
    core = at_ref[0] % CORES
    for y in range(chips):
        own_ref[y] = part_ref[y * CORES + core]
        other_ref[y] = part_ref[y * CORES + 1 - core]


def passage_part(at, dscore, queries, peers):
    pieces, _, step = queries.shape
    width = pieces * step // peers
    smem = pl.BlockSpec(memory_space=pltpu.SMEM)
    vmem = pl.BlockSpec(memory_space=pltpu.VMEM)
    half = jax.ShapeDtypeStruct((peers // CORES, dscore.shape[0], width), B16)
    return pl.pallas_call(
        passage_part_kernel,
        in_specs=[smem, vmem, pl.BlockSpec(memory_space=pl.ANY)],
        out_specs=[vmem, vmem],
        out_shape=[half, half],
        scratch_shapes=[
            pltpu.VMEM(queries.shape, B16),
            pltpu.VMEM((peers, dscore.shape[0], width), B16),
        ],
        compiler_params=params(16),
        name="passage_part",
    )(at, dscore, queries)


def pair_sum_kernel(at_ref, own_ref, got_ref, mine_ref, *out_refs):
    chips = own_ref.shape[0]
    chip = at_ref[0] // CORES

    def pair(k):
        y = (chip + k) % chips
        return own_ref[y].astype(F32) + got_ref[y].astype(F32)

    mine_ref[...] = pair(0)
    for k in range(1, chips):
        out_refs[k - 1][...] = pair(k).astype(B16)


def pair_sum(at, own, got):
    chips, rows, width = own.shape
    vmem = pl.BlockSpec(memory_space=pltpu.VMEM)
    return pl.pallas_call(
        pair_sum_kernel,
        in_specs=[pl.BlockSpec(memory_space=pltpu.SMEM), vmem, vmem],
        out_specs=[vmem] * chips,
        out_shape=[jax.ShapeDtypeStruct((rows, width), F32)]
        + [jax.ShapeDtypeStruct((rows, width), B16)] * (chips - 1),
        compiler_params=params(16),
        name="pair_sum",
    )(at, own, got)


def sent_to_all(value, axis):
    peers = lax.axis_size(axis)
    return lax.all_to_all(
        jnp.broadcast_to(value[None], (peers, *value.shape)), axis, 0, 0, tiled=True
    )


def exchanged(block, experts):
    rows, width = block.shape
    got = lax.all_to_all(
        block.reshape(experts, rows // experts, width), ("row", "col"), 0, 0, tiled=True
    )
    return got.reshape(rows, width)


def shards(
    question_vectors,
    document_vectors,
    positive,
    tokens,
    expert_ids,
    route_weights,
    expert_gate_up,
    expert_down,
):
    row_size = lax.axis_size("row")
    col_size = lax.axis_size("col")
    experts = row_size * col_size
    gate_up, down = expert_gate_up[0], expert_down[0]
    hidden = down.shape[0]

    ids_t, weights_t = expert_ids.T, route_weights.T
    tokens_out = send_tokens(ids_t, tokens, experts)

    passages = lax.all_gather(document_vectors, "row")
    queries = sent_to_all(question_vectors, "col")
    scores, stat = local_scores(queries, passages)
    stats = sent_to_all(stat, "col")
    at = lax.axis_index("col") * scores.shape[0]
    stats, tokens_out = lax.optimization_barrier((stats, tokens_out))
    part, dscore = query_part(at[None], scores, stats, positive[None], passages)
    parts = lax.all_to_all(
        part.reshape(col_size, -1, part.shape[1]), "col", 0, 0, tiled=True
    )
    row = lax.axis_index("row")[None]
    own, other = passage_part(row, dscore, queries, row_size)
    got = lax.ppermute(other, "row", [(i, i ^ 1) for i in range(row_size)])
    mine, *further = pair_sum(row, own, got)
    further = [
        lax.ppermute(
            value, "row", [(i, (i + k * CORES) % row_size) for i in range(row_size)]
        )
        for k, value in enumerate(further, 1)
    ]
    tokens_out, *further = lax.optimization_barrier((tokens_out, *further))
    passage_grad = mine + sum(value.astype(F32) for value in further)
    slot_inputs = exchanged(tokens_out, experts)
    grads_out, cot = send_grads(ids_t, weights_t, parts, experts)
    slot_grads = exchanged(grads_out, experts)

    plan = combine_plan(expert_ids, experts)
    hid, cg, cu, inputs9 = forward(slot_inputs, gate_up, hidden)
    passage_grad, cg, plan = lax.optimization_barrier((passage_grad, cg, plan))
    back_out, pre_grad, grads9 = backward(slot_grads, down, cg, cu, gate_up)
    returned = exchanged(back_out, experts)
    down_grad = weight_grad(hid, hid, slot_grads, grads9, down.shape[1], MAIN, 0, "down_grad")
    gate_up_grad = weight_grad(
        slot_inputs, inputs9, pre_grad, pre_grad, 2 * hidden, 0, MAIN, "gate_up_grad", True
    )
    token_grad = combine(plan, cot, returned)
    return (passage_grad, token_grad, gate_up_grad[None], down_grad[None])


def solution(mesh):
    in_specs = (
        P("row", "col"),
        P("col", "row"),
        P("row"),
        P(("row", "col"), None),
        P(("row", "col"), None),
        P(("row", "col"), None),
        P(("row", "col"), None, None),
        P(("row", "col"), None, None),
    )
    out_specs = (
        P("col", "row"),
        P(("row", "col"), None),
        P(("row", "col"), None, None),
        P(("row", "col"), None, None),
    )
    return jax.shard_map(shards, mesh=mesh, in_specs=in_specs, out_specs=out_specs, check_vma=False)
```

```python
import functools

import jax
import jax.numpy as jnp
from jax import lax
from jax.experimental import pallas as pl
from jax.experimental.pallas import tpu as pltpu
from jax.sharding import PartitionSpec as P

SEQ_LEN = 8
SHARPNESS = 0.02
MAIN = 8
LANES = 128
B16 = jnp.bfloat16
F32 = jnp.float32


def iota(shape, dim):
    return lax.broadcasted_iota(jnp.int32, shape, dim)


def params(mib=56):
    return pltpu.CompilerParams(vmem_limit_bytes=mib * 1024 * 1024)


def whole(shape):
    zeros = (0,) * len(shape)
    return pl.BlockSpec(shape, lambda *_: zeros, pipeline_mode=pl.Buffered(1))


def dot(a, b, dims=((1,), (0,))):
    return lax.dot_general(a, b, (dims, ((), ())), preferred_element_type=F32)


def one_hot(mask):
    return jnp.where(mask, 1.0, 0.0).astype(B16)


def slot_keys(ids_t, experts):
    toks = ids_t.shape[1]
    expert = iota((experts, toks), 0)
    hit = jnp.zeros((experts, toks), F32)
    for k in range(ids_t.shape[0]):
        hit += jnp.where(ids_t[k : k + 1, :] == expert, 1.0, 0.0)
    earlier = one_hot(iota((toks, toks), 0) < iota((toks, toks), 1))
    rank = dot(hit.astype(B16), earlier)
    return jnp.where(hit > 0.0, rank, -1.0).astype(jnp.int32)


def per_slot(value):
    experts, toks = value.shape
    return jnp.broadcast_to(value[:, None, :], (experts, MAIN, toks)).reshape(
        experts * MAIN, toks
    )


def fold_up(ninth, fold_ref):
    experts, depth = ninth.shape
    width = depth // MAIN
    for half in range(width // LANES):
        for i in range(MAIN):
            start = i * width + half * LANES
            fold_ref[half, pl.ds(i, experts, stride=MAIN), :] = ninth[:, start : start + LANES]


def write_fold(fold_ref, out_ref):
    for half in range(fold_ref.shape[0]):
        out_ref[:, half * LANES : (half + 1) * LANES] = fold_ref[half].astype(B16)


def send_tokens_kernel(ids_ref, tok_ref, out_ref, mask_ref, fold_ref):
    j = pl.program_id(0)
    tiles = pl.num_programs(0) - 1
    width = out_ref.shape[1]
    experts = out_ref.shape[0] // MAIN

    @pl.when(j == 0)
    def _():
        key = slot_keys(ids_ref[...], experts)
        slot = iota(mask_ref.shape, 0) % MAIN
        mask_ref[...] = one_hot(per_slot(key) == slot)
        fold_up(dot(one_hot(key == MAIN), tok_ref[...]), fold_ref)

    @pl.when(j < tiles)
    def _():
        cols = pl.ds(pl.multiple_of(j * width, width), width)
        out_ref[...] = dot(mask_ref[...], tok_ref[:, cols]).astype(B16)

    @pl.when(j == tiles)
    def _():
        write_fold(fold_ref, out_ref)


def send_tokens(ids_t, tokens, experts):
    toks, depth = tokens.shape
    width = depth // MAIN
    rows = experts * MAIN
    return pl.pallas_call(
        send_tokens_kernel,
        grid=(MAIN + 1,),
        in_specs=[whole(ids_t.shape), whole(tokens.shape)],
        out_specs=pl.BlockSpec((rows, width), lambda j: (0, j)),
        out_shape=jax.ShapeDtypeStruct((rows, depth + width), B16),
        scratch_shapes=[
            pltpu.VMEM((rows, toks), B16),
            pltpu.VMEM((width // LANES, rows, LANES), F32),
        ],
        compiler_params=params(24),
        name="send_tokens",
    )(ids_t, tokens)


def send_grads_kernel(
    ids_ref, weight_ref, part_hbm, out_ref, cot_ref, mask_ref, row_ref, rep_ref, fold_ref, part_ref
):
    j = pl.program_id(0)
    tiles = pl.num_programs(0) - 1
    width = out_ref.shape[1]
    experts = out_ref.shape[0] // MAIN
    slots, toks = mask_ref.shape

    @pl.when(j == 0)
    def _():
        pltpu.sync_copy(part_hbm, part_ref)
        ids = ids_ref[...]
        key = slot_keys(ids, experts)
        expert = iota((experts, toks), 0)
        weight = jnp.zeros((experts, toks), F32)
        for k in range(ids.shape[0]):
            weight += jnp.where(ids[k : k + 1, :] == expert, weight_ref[k : k + 1, :], 0.0)
        mine = per_slot(key) == iota((slots, toks), 0) % MAIN
        mask_ref[...] = one_hot(mine)
        row_ref[...] = jnp.sum(jnp.where(mine, per_slot(weight), 0.0), axis=1, keepdims=True)
        total = part_ref[0].astype(F32)
        for c in range(1, part_ref.shape[0]):
            total += part_ref[c].astype(F32)
        cot = (total / SEQ_LEN).astype(B16)
        cot_ref[...] = cot
        spread = one_hot(iota((toks, cot.shape[0]), 0) // SEQ_LEN == iota((toks, cot.shape[0]), 1))
        rep_ref[...] = dot(spread, cot).astype(B16)
        last = key == MAIN
        ninth = jnp.sum(jnp.where(last, weight, 0.0), axis=1, keepdims=True)
        fold_up(dot(one_hot(last), rep_ref[...]) * ninth, fold_ref)

    @pl.when(j < tiles)
    def _():
        cols = pl.ds(pl.multiple_of(j * width, width), width)
        out_ref[...] = (dot(mask_ref[...], rep_ref[:, cols]) * row_ref[...]).astype(B16)

    @pl.when(j == tiles)
    def _():
        write_fold(fold_ref, out_ref)


def send_grads(ids_t, weights_t, parts, experts):
    toks = ids_t.shape[1]
    _, queries, depth = parts.shape
    width = depth // MAIN
    rows = experts * MAIN
    return pl.pallas_call(
        send_grads_kernel,
        grid=(MAIN + 1,),
        in_specs=[
            whole(ids_t.shape),
            whole(weights_t.shape),
            pl.BlockSpec(memory_space=pl.ANY),
        ],
        out_specs=[
            pl.BlockSpec((rows, width), lambda j: (0, j)),
            pl.BlockSpec((queries, depth), lambda j: (0, 0)),
        ],
        out_shape=[
            jax.ShapeDtypeStruct((rows, depth + width), B16),
            jax.ShapeDtypeStruct((queries, depth), B16),
        ],
        scratch_shapes=[
            pltpu.VMEM((rows, toks), B16),
            pltpu.VMEM((rows, 1), F32),
            pltpu.VMEM((toks, depth), B16),
            pltpu.VMEM((width // LANES, rows, LANES), F32),
            pltpu.VMEM(parts.shape, B16),
        ],
        compiler_params=params(24),
        name="send_grads",
    )(ids_t, weights_t, parts)


def unfold(fold, fold_ref, out_ref):
    sources, depth = out_ref.shape
    width = depth // MAIN
    for half in range(width // LANES):
        at = slice(half * LANES, (half + 1) * LANES)
        fold_ref[half] = fold[:, at].astype(F32)
        for i in range(MAIN):
            piece = fold_ref[half, pl.ds(i, sources, stride=MAIN), :]
            start = i * width + half * LANES
            out_ref[:, start : start + LANES] = piece.astype(B16)


def forward_kernel(x_ref, gate_ref, up_ref, hid_ref, cg_ref, cu_ref, x9_ref, fold_ref):
    j = pl.program_id(0)
    depth = gate_ref.shape[0]
    rows = x_ref.shape[0]

    @pl.when(j == 0)
    def _():
        unfold(x_ref[:, depth:], fold_ref, x9_ref)

    def finish(at, gate, up):
        sig = 1.0 / (1.0 + jnp.exp(-gate))
        act = gate * sig
        hid_ref[at, :] = (act * up).astype(B16)
        cg_ref[at, :] = (up * (sig * (1.0 + gate * (1.0 - sig)))).astype(B16)
        cu_ref[at, :] = act.astype(B16)

    step = rows // 4
    for m in range(4):
        x = x_ref[m * step : (m + 1) * step, :depth]
        finish(slice(m * step, (m + 1) * step), dot(x, gate_ref[...]), dot(x, up_ref[...]))
    x = x9_ref[...]
    finish(slice(rows, hid_ref.shape[0]), dot(x, gate_ref[...]), dot(x, up_ref[...]))


def forward(x, gate_up, hidden):
    rows, _ = x.shape
    depth = gate_up.shape[0]
    sources = rows // MAIN
    tile = 256
    tiles = hidden // tile
    col = lambda j: (0, j)
    part = pl.BlockSpec((rows + sources, tile), col)
    shape = jax.ShapeDtypeStruct((rows + sources, hidden), B16)
    return pl.pallas_call(
        forward_kernel,
        grid=(tiles,),
        in_specs=[
            whole(x.shape),
            pl.BlockSpec((depth, tile), col),
            pl.BlockSpec((depth, tile), lambda j: (0, j + tiles)),
        ],
        out_specs=[part, part, part, pl.BlockSpec((sources, depth), lambda j: (0, 0))],
        out_shape=[shape, shape, shape, jax.ShapeDtypeStruct((sources, depth), B16)],
        scratch_shapes=[pltpu.VMEM((depth // MAIN // LANES, rows, LANES), F32)],
        compiler_params=params(),
        cost_estimate=pl.CostEstimate(
            flops=2 * (rows + sources) * depth * 2 * hidden,
            bytes_accessed=2 * (x.size + gate_up.size + 3 * (rows + sources) * hidden),
            transcendentals=(rows + sources) * hidden,
        ),
        name="expert_forward",
    )(x, gate_up, gate_up)


CHUNKS = 4


def backward_kernel(
    first, *refs
):
    g_refs, refs = refs[:CHUNKS], refs[CHUNKS:]
    down_ref, cg_ref, cu_ref, w_ref, out_ref, pair_ref, g9_ref, pg_ref, fold_ref = refs
    j = pl.program_id(0)
    step = g_refs[0].shape[0]
    rows = step * CHUNKS
    sources, depth = g9_ref.shape
    width = out_ref.shape[1]
    total = rows + sources
    tile = down_ref.shape[0]
    hidden = pg_ref.shape[1] // 2


    @pl.when(j == 0)
    def _():
        unfold(jnp.concatenate([g[:, depth:] for g in g_refs]), fold_ref, g9_ref)

    @pl.when(j < first)
    def _():
        def finish(at, grad):
            gate_cols = pl.ds(pl.multiple_of(j * tile, tile), tile)
            up_cols = pl.ds(pl.multiple_of(hidden + j * tile, tile), tile)
            gate = (grad * cg_ref[at, :].astype(F32)).astype(B16)
            up = (grad * cu_ref[at, :].astype(F32)).astype(B16)
            pg_ref[at, gate_cols] = gate
            pg_ref[at, up_cols] = up
            pair_ref[at, :tile] = gate
            pair_ref[at, tile:] = up

        for m in range(CHUNKS):
            at = slice(m * step, (m + 1) * step)
            finish(at, dot(g_refs[m][:, :depth], down_ref[...], ((1,), (1,))))
        finish(slice(rows, total), dot(g9_ref[...], down_ref[...], ((1,), (1,))))

    @pl.when((j >= first) & (j < first + MAIN))
    def _():
        grads = dot(pg_ref[...], w_ref[...], ((1,), (1,)))
        out_ref[...] = grads[:rows].astype(B16)
        ninth = grads[rows:]
        for half in range(width // LANES):
            fold_ref[half, pl.ds(j - first, sources, stride=MAIN), :] = ninth[
                :, half * LANES : (half + 1) * LANES
            ]

    @pl.when(j == first + MAIN)
    def _():
        for half in range(width // LANES):
            out_ref[:, half * LANES : (half + 1) * LANES] = fold_ref[half].astype(B16)


def backward(g, down, cg, cu, gate_up):
    rows, _ = g.shape
    hidden, depth = down.shape
    sources = rows // MAIN
    width = depth // MAIN
    tile = 256
    first = hidden // tile
    head = lambda j: (0, jnp.minimum(j, first - 1))
    part = pl.BlockSpec((rows + sources, tile), head)
    return pl.pallas_call(
        functools.partial(backward_kernel, first),
        grid=(first + MAIN + 1,),
        in_specs=[
            *[
                pl.BlockSpec(
                    (rows // CHUNKS, g.shape[1]),
                    lambda j, m=m: (m, 0),
                    pipeline_mode=pl.Buffered(1),
                )
                for m in range(CHUNKS)
            ],
            pl.BlockSpec((tile, depth), lambda j: (jnp.minimum(j, first - 1), 0)),
            part,
            part,
            pl.BlockSpec(
                (width, 2 * hidden), lambda j: (jnp.clip(j - first, 0, MAIN - 1), 0)
            ),
        ],
        out_specs=[
            pl.BlockSpec((rows, width), lambda j: (0, jnp.maximum(j - first, 0))),
            pl.BlockSpec((rows + sources, 2 * tile), head),
            pl.BlockSpec((sources, depth), lambda j: (0, 0)),
        ],
        out_shape=[
            jax.ShapeDtypeStruct((rows, depth + width), B16),
            jax.ShapeDtypeStruct((rows + sources, 2 * hidden), B16),
            jax.ShapeDtypeStruct((sources, depth), B16),
        ],
        scratch_shapes=[
            pltpu.VMEM((rows + sources, 2 * hidden), B16),
            pltpu.VMEM((width // LANES, rows, LANES), F32),
        ],
        compiler_params=params(),
        cost_estimate=pl.CostEstimate(
            flops=6 * (rows + sources) * depth * hidden,
            bytes_accessed=2 * (2 * g.size + down.size + gate_up.size),
            transcendentals=0,
        ),
        name="expert_backward",
    )(*[g] * CHUNKS, down, cg, cu, gate_up)


def weight_grad_kernel(a_ref, a9_ref, b_ref, b9_ref, out_ref):
    rows = b_ref.shape[0]
    width = out_ref.shape[0]
    out_ref[...] = (
        dot(a_ref[:, :width], b_ref[...], ((0,), (0,))) + dot(a9_ref[...], b9_ref[...], ((0,), (0,)))
    ).astype(B16)


def weight_grad(a, a9, b, b9, columns, a9_block, b9_block, name, pairs=False):
    sources = a9.shape[0] if a9_block == 0 else a.shape[0] - 8 * (a.shape[0] // 9)
    rows = sources * MAIN
    width = a9.shape[1]
    tile = 256
    half = columns // tile // 2
    place = (lambda j: (0, j // 2 + (j % 2) * half)) if pairs else (lambda j: (0, j))
    return pl.pallas_call(
        weight_grad_kernel,
        grid=(columns // tile,),
        in_specs=[
            pl.BlockSpec((rows, a.shape[1]), lambda j: (0, 0), pipeline_mode=pl.Buffered(1)),
            pl.BlockSpec(
                (sources, width), lambda j: (a9_block, 0), pipeline_mode=pl.Buffered(1)
            ),
            pl.BlockSpec((rows, tile), lambda j: (0, j)),
            pl.BlockSpec((sources, tile), lambda j: (b9_block, j)),
        ],
        out_specs=pl.BlockSpec((width, tile), place),
        out_shape=jax.ShapeDtypeStruct((width, columns), B16),
        compiler_params=params(),
        cost_estimate=pl.CostEstimate(
            flops=2 * 9 * sources * width * columns,
            bytes_accessed=2 * (9 * sources * (width + columns) + width * columns),
            transcendentals=0,
        ),
        name=name,
    )(a, a9, b, b9)


def plan_kernel(ids_ref, mask_ref, last_ref):
    toks, slots = mask_ref.shape
    experts = slots // MAIN
    ids = ids_ref[...]
    expert = iota((toks, experts), 1)
    hit = jnp.zeros((toks, experts), F32)
    for k in range(ids.shape[1]):
        hit += jnp.where(ids[:, k : k + 1] == expert, 1.0, 0.0)
    earlier = one_hot(iota((toks, toks), 1) < iota((toks, toks), 0))
    rank = dot(earlier, hit.astype(B16))
    key = jnp.where(hit > 0.0, rank, -1.0)
    last_ref[...] = one_hot(key == float(MAIN))
    spread = one_hot(iota((experts, slots), 0) == iota((experts, slots), 1) // MAIN)
    slot = (iota((toks, slots), 1) % MAIN).astype(F32)
    mask_ref[...] = one_hot(dot(key.astype(B16), spread) == slot)


def combine_plan(ids, experts):
    toks = ids.shape[0]
    return pl.pallas_call(
        plan_kernel,
        out_shape=[
            jax.ShapeDtypeStruct((toks, experts * MAIN), B16),
            jax.ShapeDtypeStruct((toks, experts), B16),
        ],
        compiler_params=params(16),
        name="combine_plan",
    )(ids)


def combine_kernel(mask_ref, last_ref, cot_ref, got_ref, fold_ref, out_ref, ninth_ref, buf_ref):
    j = pl.program_id(0)
    toks = mask_ref.shape[0]
    width = out_ref.shape[1]

    @pl.when(j == 0)
    def _():
        unfold(fold_ref[...], buf_ref, ninth_ref)

    queries = cot_ref.shape[0]
    spread = one_hot(iota((toks, queries), 0) // SEQ_LEN == iota((toks, queries), 1))
    cols = pl.ds(pl.multiple_of(j * width, width), width)
    total = dot(mask_ref[...], got_ref[...]) + dot(last_ref[...], ninth_ref[:, cols])
    out_ref[...] = (dot(spread, cot_ref[...]) + total).astype(B16)


def combine(plan, cot, got):
    mask, last = plan
    toks, experts = last.shape
    queries, depth = cot.shape
    rows = got.shape[0]
    fold = depth // MAIN
    width = 4 * fold
    return pl.pallas_call(
        combine_kernel,
        grid=(depth // width,),
        in_specs=[
            whole(mask.shape),
            whole(last.shape),
            pl.BlockSpec((queries, width), lambda j: (0, j)),
            pl.BlockSpec((rows, width), lambda j: (0, j)),
            pl.BlockSpec((rows, fold), lambda j: (0, MAIN), pipeline_mode=pl.Buffered(1)),
        ],
        out_specs=pl.BlockSpec((toks, width), lambda j: (0, j)),
        out_shape=jax.ShapeDtypeStruct((toks, depth), B16),
        scratch_shapes=[
            pltpu.VMEM((experts, depth), B16),
            pltpu.VMEM((fold // LANES, rows, LANES), F32),
        ],
        compiler_params=params(32),
        name="combine",
    )(mask, last, cot, got, got)


def scores_kernel(query_hbm, passage_ref, score_ref, stat_ref, query_ref):
    pltpu.sync_copy(query_hbm, query_ref)
    pieces, _, width = passage_ref.shape
    step = query_ref.shape[2]
    total = jnp.zeros(score_ref.shape, F32)
    for r in range(pieces):
        for h in range(width // step):
            part = passage_ref[r, :, h * step : (h + 1) * step]
            total += dot(part, query_ref[r * (width // step) + h], ((1,), (1,)))
    scores = total / SHARPNESS
    peak = jnp.max(scores, axis=0, keepdims=True)
    mass = jnp.sum(jnp.exp(scores - peak), axis=0, keepdims=True)
    score_ref[...] = scores
    stat_ref[...] = jnp.where(iota(stat_ref.shape, 0) == 0, peak, mass)


def local_scores(queries, passages):
    shape = (passages.shape[1], queries.shape[1])
    return pl.pallas_call(
        scores_kernel,
        in_specs=[pl.BlockSpec(memory_space=pl.ANY), pl.BlockSpec(memory_space=pltpu.VMEM)],
        scratch_shapes=[pltpu.VMEM(queries.shape, B16)],
        out_shape=[
            jax.ShapeDtypeStruct(shape, F32),
            jax.ShapeDtypeStruct((2, shape[1]), F32),
        ],
        compiler_params=params(16),
        name="local_scores",
    )(queries, passages)


def query_part_kernel(
    at_ref, score_ref, stat_hbm, pos_ref, passage_ref, out_ref, dscore_ref, stat_ref
):
    pltpu.sync_copy(stat_hbm, stat_ref)
    parts = [stat_ref[c] for c in range(stat_ref.shape[0])]
    peak = functools.reduce(jnp.maximum, [p[0:1] for p in parts])
    mass = sum(p[1:2] * jnp.exp(p[0:1] - peak) for p in parts)
    column = at_ref[0] + iota(score_ref.shape, 0)
    chosen = jnp.where(pos_ref[...] == column, 1.0, 0.0)
    soft = jnp.exp(score_ref[...] - peak) / mass
    dscore = ((soft - chosen) / SHARPNESS).astype(B16)
    dscore_ref[...] = dscore
    pieces, _, width = passage_ref.shape
    for r in range(pieces):
        out_ref[:, r * width : (r + 1) * width] = dot(
            dscore, passage_ref[r], ((0,), (0,))
        ).astype(B16)


def query_part(at, scores, stats, positive, passages):
    pieces, _, width = passages.shape
    smem = pl.BlockSpec(memory_space=pltpu.SMEM)
    vmem = pl.BlockSpec(memory_space=pltpu.VMEM)
    return pl.pallas_call(
        query_part_kernel,
        in_specs=[smem, vmem, pl.BlockSpec(memory_space=pl.ANY), vmem, vmem],
        out_specs=[vmem] * 2,
        scratch_shapes=[pltpu.VMEM(stats.shape, F32)],
        out_shape=[
            jax.ShapeDtypeStruct((scores.shape[1], pieces * width), B16),
            jax.ShapeDtypeStruct(scores.shape, B16),
        ],
        compiler_params=params(16),
        name="query_part",
    )(at, scores, stats, positive, passages)


CORES = 2


def passage_part_kernel(at_ref, dscore_ref, query_hbm, own_ref, other_ref, query_ref, part_ref):
    pltpu.sync_copy(query_hbm, query_ref)
    chips, _, width = own_ref.shape
    pieces, _, step = query_ref.shape
    for c in range(pieces):
        at = c * step
        part_ref[at // width, :, at % width : at % width + step] = dot(
            dscore_ref[...], query_ref[c]
        ).astype(B16)
    core = at_ref[0] % CORES
    for y in range(chips):
        own_ref[y] = part_ref[y * CORES + core]
        other_ref[y] = part_ref[y * CORES + 1 - core]


def passage_part(at, dscore, queries, peers):
    pieces, _, step = queries.shape
    width = pieces * step // peers
    smem = pl.BlockSpec(memory_space=pltpu.SMEM)
    vmem = pl.BlockSpec(memory_space=pltpu.VMEM)
    half = jax.ShapeDtypeStruct((peers // CORES, dscore.shape[0], width), B16)
    return pl.pallas_call(
        passage_part_kernel,
        in_specs=[smem, vmem, pl.BlockSpec(memory_space=pl.ANY)],
        out_specs=[vmem, vmem],
        out_shape=[half, half],
        scratch_shapes=[
            pltpu.VMEM(queries.shape, B16),
            pltpu.VMEM((peers, dscore.shape[0], width), B16),
        ],
        compiler_params=params(16),
        name="passage_part",
    )(at, dscore, queries)


def pair_sum_kernel(at_ref, own_ref, got_ref, mine_ref, *out_refs):
    chips = own_ref.shape[0]
    chip = at_ref[0] // CORES

    def pair(k):
        y = (chip + k) % chips
        return own_ref[y].astype(F32) + got_ref[y].astype(F32)

    mine_ref[...] = pair(0)
    for k in range(1, chips):
        out_refs[k - 1][...] = pair(k).astype(B16)


def pair_sum(at, own, got):
    chips, rows, width = own.shape
    vmem = pl.BlockSpec(memory_space=pltpu.VMEM)
    return pl.pallas_call(
        pair_sum_kernel,
        in_specs=[pl.BlockSpec(memory_space=pltpu.SMEM), vmem, vmem],
        out_specs=[vmem] * chips,
        out_shape=[jax.ShapeDtypeStruct((rows, width), F32)]
        + [jax.ShapeDtypeStruct((rows, width), B16)] * (chips - 1),
        compiler_params=params(16),
        name="pair_sum",
    )(at, own, got)


def sent_to_all(value, axis):
    peers = lax.axis_size(axis)
    return lax.all_to_all(
        jnp.broadcast_to(value[None], (peers, *value.shape)), axis, 0, 0, tiled=True
    )


def exchanged(block, experts):
    rows, width = block.shape
    got = lax.all_to_all(
        block.reshape(experts, rows // experts, width), ("row", "col"), 0, 0, tiled=True
    )
    return got.reshape(rows, width)


def shards(
    question_vectors,
    document_vectors,
    positive,
    tokens,
    expert_ids,
    route_weights,
    expert_gate_up,
    expert_down,
):
    row_size = lax.axis_size("row")
    col_size = lax.axis_size("col")
    experts = row_size * col_size
    gate_up, down = expert_gate_up[0], expert_down[0]
    hidden = down.shape[0]

    ids_t, weights_t = expert_ids.T, route_weights.T
    tokens_out = send_tokens(ids_t, tokens, experts)

    passages = lax.all_gather(document_vectors, "row")
    queries = sent_to_all(question_vectors, "col")
    scores, stat = local_scores(queries, passages)
    stats = sent_to_all(stat, "col")
    at = lax.axis_index("col") * scores.shape[0]
    stats, tokens_out = lax.optimization_barrier((stats, tokens_out))
    part, dscore = query_part(at[None], scores, stats, positive[None], passages)
    parts = lax.all_to_all(
        part.reshape(col_size, -1, part.shape[1]), "col", 0, 0, tiled=True
    )
    row = lax.axis_index("row")[None]
    own, other = passage_part(row, dscore, queries, row_size)
    got = lax.ppermute(other, "row", [(i, i ^ 1) for i in range(row_size)])
    mine, *further = pair_sum(row, own, got)
    tokens_out, mine, *further = lax.optimization_barrier((tokens_out, mine, *further))
    slot_inputs = exchanged(tokens_out, experts)
    grads_out, cot = send_grads(ids_t, weights_t, parts, experts)
    grads_out, *further = lax.optimization_barrier((grads_out, *further))
    further = [
        lax.ppermute(
            value, "row", [(i, (i + k * CORES) % row_size) for i in range(row_size)]
        )
        for k, value in enumerate(further, 1)
    ]
    grads_out, *further = lax.optimization_barrier((grads_out, *further))
    passage_grad = mine + sum(value.astype(F32) for value in further)
    slot_grads = exchanged(grads_out, experts)

    plan = combine_plan(expert_ids, experts)
    hid, cg, cu, inputs9 = forward(slot_inputs, gate_up, hidden)
    passage_grad, cg, plan = lax.optimization_barrier((passage_grad, cg, plan))
    back_out, pre_grad, grads9 = backward(slot_grads, down, cg, cu, gate_up)
    returned = exchanged(back_out, experts)
    down_grad = weight_grad(hid, hid, slot_grads, grads9, down.shape[1], MAIN, 0, "down_grad")
    gate_up_grad = weight_grad(
        slot_inputs, inputs9, pre_grad, pre_grad, 2 * hidden, 0, MAIN, "gate_up_grad", True
    )
    token_grad = combine(plan, cot, returned)
    return (passage_grad, token_grad, gate_up_grad[None], down_grad[None])


def solution(mesh):
    in_specs = (
        P("row", "col"),
        P("col", "row"),
        P("row"),
        P(("row", "col"), None),
        P(("row", "col"), None),
        P(("row", "col"), None),
        P(("row", "col"), None, None),
        P(("row", "col"), None, None),
    )
    out_specs = (
        P("col", "row"),
        P(("row", "col"), None),
        P(("row", "col"), None, None),
        P(("row", "col"), None, None),
    )
    return jax.shard_map(shards, mesh=mesh, in_specs=in_specs, out_specs=out_specs, check_vma=False)
```
